32 devices in a mesh: grp: 2 (over y), mesh: 16 (over z, x, core).
Axes of the slice: x: 2, y: 2, z: 4, core: 2. Of those that a mesh axis runs over, the one named last changes fastest.
Arguments:
- basis: bfloat16 [65536, 512], P(('grp', 'mesh')), parts along dimension 0, may hold values from -6 to 6
- blocks: bfloat16 [2, 512, 3, 128, 128], P(None, ('grp', 'mesh')), parts along dimension 1, may hold values from -0.0017089844 to 0.0017089844
- columns: int32 [2, 512, 2], P(None, ('grp', 'mesh')), parts along dimension 1, may hold values from 0 to 31
- sends: int32 [32, 16], P(('grp', 'mesh')), parts along dimension 0, may hold values from 0 to 15
Outputs:
- projected: float32 [1024, 1024], P(('grp', 'mesh')), parts along dimension 0
The draws below stay inside these ranges and needn't reach their ends.
There are 2 independent parts, one for each index of `grp`. The reference program is written for one: setup_inputs(seed, part) draws one part's arguments, and reference() takes and returns one part's arrays. A program takes and returns all parts, laid end to end along the dimension named above; each array names one. Nothing has to cross between parts.
All inputs are finite; a program needn't handle non-finite values.
Results may differ from the reference program's by a relative error of at most 0.0029.
Values may be sent and summed in bfloat16 or wider, within the bound.
A program may use at most 64 MiB of HBM per device.

```python
import jax
import jax.numpy as jnp
from jax import lax

BLOCK = 128
BASIS = 512
PARAMS = 2
ROWBLK = 16
SLOTS = 3
HALO = 8
NROWB = 256
NROWS = 32768
N_MESH = 16


def plant(values, own_key, smallest, largest):
    place = [jax.random.randint(jax.random.fold_in(own_key, axis), (), 0, length) for axis, length in enumerate(values.shape)]
    main_axis = values.shape.index(max(values.shape))
    beside = place[:main_axis] + [(place[main_axis] + 1) % values.shape[main_axis]] + place[main_axis + 1:]
    return values.at[tuple(place)].set(smallest).at[tuple(beside)].set(largest)


def with_spikes(drawn, key, source, target, blocks, factor):
    owner, partner = [(jnp.arange(drawn.shape[position]) // (drawn.shape[position] // blocks)).reshape([-1 if axis == position else 1 for axis in range(drawn.ndim)]) for position in (source, target)]
    chosen = jax.random.permutation(key, blocks)[partner]
    strong = (owner == chosen) | (owner == (partner + blocks // 2) % blocks)
    return jnp.where(strong, factor * drawn, drawn)


def block_scale(key, shape, shards, least, high):
    factor_of, own = 1.0, jax.random.fold_in(key, 6)
    for dim, shards_of in shards:
        heights = jnp.exp(jax.random.uniform(jax.random.fold_in(own, dim), (shards_of,), jnp.float32, least / len(shards), high / len(shards)))
        factor_of = factor_of * jnp.repeat(heights, shape[dim] // shards_of).reshape([-1 if axis == dim else 1 for axis in range(len(shape))])
    return factor_of


def bell_draw(rng, shape, deviation, reach, pieces=(), kind=jnp.bfloat16):
    drawn = deviation * jax.random.normal(rng, shape, jnp.float32)
    if pieces:
        drawn = drawn * block_scale(rng, shape, pieces, -0.22, 0.18)
    return jnp.clip(drawn, -reach, reach).astype(kind)


def heavy_noise(own_key, extent, scale, bound, cuts, heavy, held_as=jnp.bfloat16):
    drawn = scale * jax.random.normal(own_key, extent, jnp.float32)
    if cuts:
        drawn = drawn * block_scale(own_key, extent, cuts, -0.22, 0.18)
    return jnp.clip(with_spikes(drawn, jax.random.fold_in(own_key, 3), *heavy), -bound, bound).astype(held_as)


def setup_inputs(seed: int = 0, part: int = 0) -> dict:
    seeds = jax.random.split(jax.random.key(seed), 5)
    own_keys = jax.random.split(jax.random.fold_in(seeds[4], part), 5)
    return {
        "basis": heavy_noise(own_keys[0], (NROWS, BASIS), 1.0, 6.0, ((0, 16),), (0, 1, 16, 2.0)),
        "blocks": bell_draw(own_keys[1], (PARAMS, NROWB, SLOTS, BLOCK, BLOCK), (SLOTS * BLOCK * NROWS) ** -0.5, 0.0017089844, ((1, 16),)),
        "columns": plant(jax.random.randint(own_keys[2], (PARAMS, NROWB, SLOTS - 1), 0, ROWBLK + 2 * HALO), jax.random.fold_in(own_keys[2], 1), 0, (ROWBLK + 2 * HALO) - 1).astype(jnp.int32),
        "sends": plant(jax.random.randint(own_keys[3], (N_MESH, 2 * HALO), 0, ROWBLK), jax.random.fold_in(own_keys[3], 1), 0, ROWBLK - 1).astype(jnp.int32),
    }


def take_rows(source, positions):
    return jnp.take(source, positions, axis=0)


def reference(basis, blocks, columns, sends):
    own_blocks = basis.reshape(N_MESH, ROWBLK, BLOCK, BASIS)
    picker = jax.vmap(take_rows)
    upward = picker(own_blocks, sends[:, HALO:].astype(jnp.int32))
    downward = picker(own_blocks, sends[:, :HALO].astype(jnp.int32))
    empty_rim = jnp.zeros((1, HALO, BLOCK, BASIS), basis.dtype)
    from_below = jnp.concatenate([empty_rim, upward[:-1]], axis=0)
    from_above = jnp.concatenate([downward[1:], empty_rim], axis=0)
    extended = jnp.concatenate([own_blocks, from_below, from_above], axis=1)
    diag_index = jnp.broadcast_to(jnp.arange(ROWBLK, dtype=jnp.int32)[None, :, None], (N_MESH, ROWBLK, 1))

    def project_param(param):
        slot_index = jnp.concatenate([diag_index, columns[param].reshape(N_MESH, ROWBLK, SLOTS - 1).astype(jnp.int32)], axis=2)
        param_blocks = blocks[param].reshape(N_MESH, ROWBLK, SLOTS, BLOCK, BLOCK)
        accumulated = jnp.zeros((N_MESH, ROWBLK, BLOCK, BASIS), jnp.float32)
        for slot in range(SLOTS):
            gathered = picker(extended, slot_index[:, :, slot])
            accumulated = accumulated + jnp.einsum("dbik,dbkj->dbij", param_blocks[:, :, slot].astype(jnp.float32), gathered.astype(jnp.float32))
        image_rows = accumulated.astype(jnp.bfloat16).reshape(NROWS, BASIS)
        return lax.dot_general(basis, image_rows, (((0,), (0,)), ((), ())), preferred_element_type=jnp.float32)

    return jnp.concatenate([project_param(param) for param in range(PARAMS)], axis=1)
```

```python
import functools

import jax
import jax.numpy as jnp
from jax import lax
from jax.experimental import pallas as pl
from jax.experimental.pallas import tpu as pltpu
from jax.sharding import PartitionSpec as P

MESH = pl.DeviceIdType.MESH
CORES = 2
LANES = 128
XS = 2
FAR = 1
SERVED = 3


def from_behind(value, axis, steps):
    count = lax.axis_size(axis)
    leading, last = (max(0, -steps), min(count, count - steps))
    return lax.ppermute(value, axis, [(source, source + steps) for source in range(leading, last)])


def plain_shards(basis, blocks, columns, sends):
    count_params, count_blocks, count_slots, block_size, _ = blocks.shape
    basis_width = basis.shape[1]
    halo_count = sends.shape[1] // 2
    own_blocks = basis.reshape(count_blocks, block_size, basis_width)
    diag_index = jnp.arange(count_blocks, dtype=jnp.int32)[:, None]
    images = []
    upward = jnp.take(own_blocks, sends[0, halo_count:], axis=0)
    downward = jnp.take(own_blocks, sends[0, :halo_count], axis=0)
    from_below = from_behind(upward, "mesh", 1)
    from_above = from_behind(downward, "mesh", -1)
    extended = jnp.concatenate([own_blocks, from_below, from_above], axis=0)
    for param in range(count_params):
        slot_index = jnp.concatenate([diag_index, columns[param]], axis=1)
        gathered = jnp.take(extended, slot_index, axis=0)
        accumulated = jnp.einsum(
            "bsik,bskj->bij", blocks[param], gathered, preferred_element_type=jnp.float32
        )
        images.append(
            accumulated.astype(jnp.bfloat16).reshape(count_blocks * block_size, basis_width)
        )
    stacked_images = jnp.concatenate(images, axis=1)
    return lax.psum_scatter(
        lax.dot_general(
            basis, stacked_images, (((0,), (0,)), ((), ())), preferred_element_type=jnp.float32
        ),
        "mesh",
        scatter_dimension=0,
        tiled=True,
    )


def kernel(n, zs, width, basis, blocks, columns, sends, out, *scratch):
    chunks = basis.shape[2] // width
    own, scratch = scratch[:chunks], scratch[chunks:]
    ext, scratch = scratch[:chunks], scratch[chunks:]
    (
        stage, relay, turned, ops, image, part, pair_out, pair_in, z_out, z_in, x_own, x_out, x_in, far_in,
        own_sem, ext_sem, ops_sem, halo_send, halo_recv, relay_recv, forward_send,
        pair_send, pair_recv, z_send, z_recv, x_send, x_recv, far_send, far_recv, rounds, go,
    ) = scratch
    params, count, slots, size, _ = blocks.shape
    basis_width = basis.shape[2]
    halo = sends.shape[1] // 2
    half = basis_width // 2
    each = basis_width // n
    chips = n // CORES
    plane = XS * CORES
    tall = plane * each
    last = chunks - 1
    hops = last - FAR

    me = lax.axis_index("mesh")
    core = lax.rem(me, CORES)
    chip = me // CORES
    x = lax.rem(chip, XS)
    z = chip // XS
    early = core == x
    late = core != x

    def at(z, x, core):
        return (z * XS + x) * CORES + core

    partner = at(z, x, 1 - core)
    mate = at(z, 1 - x, 1 - core)
    outer = me - 1 + 2 * core
    has_outer = jnp.logical_and(outer >= 0, outer < n)
    onward = z + 1 - 2 * x
    relayed = (
        relays_out(zs, chunks, z, 1) * x + relays_out(zs, chunks, z, 0) * (1 - x)
    )
    relaying = (
        relays_out(zs, chunks, z, 0) * x + relays_out(zs, chunks, z, 1) * (1 - x)
    )

    def local_copy(k, buffers, sems):
        return pltpu.make_async_copy(
            basis.at[:, :, pl.ds(k * width, width)], buffers[k].at[pl.ds(0, count)], sems.at[k]
        )

    ops_copy = pltpu.make_async_copy(blocks, ops, ops_sem)

    def remote(source, target, sent, received, device):
        return pltpu.make_async_remote_copy(
            src_ref=source, dst_ref=target, send_sem=sent, recv_sem=received,
            device_id={"mesh": device}, device_id_type=MESH,
        )

    def pair_halo(k):
        return remote(
            stage.at[k, core], ext[k].at[pl.ds(count + core * halo, halo)],
            halo_send.at[k, 0], halo_recv.at[k, 0], partner,
        )

    def outer_halo(k):
        return remote(
            stage.at[k, 1 - core], ext[k].at[pl.ds(count + (1 - core) * halo, halo)],
            halo_send.at[k, 1], halo_recv.at[k, 1], outer,
        )

    def relay_halo(k):
        return remote(
            stage.at[k, 1 - core], relay.at[k], halo_send.at[k, 1], relay_recv.at[k], mate
        )

    def forward_halo(k):
        return remote(
            relay.at[k], ext[k].at[pl.ds(count + core * halo, halo)],
            forward_send.at[k], halo_recv.at[k, 1], at(onward, x, core),
        )

    def pair_copy(k, h):
        return remote(
            pair_out.at[k, pl.ds(h * half, half)], pair_in.at[k, pl.ds(h * half, half)],
            pair_send.at[k, h], pair_recv.at[k, h], partner,
        )

    def z_copy(k, step):
        target = lax.rem(z + step, zs)
        return remote(
            z_out.at[k, pl.ds(target * tall, tall)], z_in.at[k, step - 1],
            z_send.at[k], z_recv.at[k], at(target, x, core),
        )

    def z_all(k):
        came = z_in.at[k, pl.ds(0, zs - 1)]
        return remote(came, came, z_send.at[k], z_recv.at[k], partner)

    def x_copy(k, which):
        to_x = x if which == 2 else 1 - x
        to_core = core if which == 1 else 1 - core
        slot = 0 if which == 2 else 1
        return remote(
            x_out.at[k, pl.ds((to_x * CORES + to_core) * each, each)], x_in.at[k, slot],
            x_send.at[k], x_recv.at[k, slot], at(z, to_x, to_core),
        )

    def far_copy(k, d):
        slot = lax.rem(chip - d // CORES + 2 * chips - 1, chips)
        return remote(
            z_out.at[k, pl.ds(d * each, each)], far_in.at[k - hops, slot],
            far_send.at[k - hops], far_recv.at[k - hops], d,
        )

    near = [(None, partner), (None, mate), (z > 0, at(z - 1, x, core)), (z < zs - 1, at(z + 1, x, core))]
    near_count = 2 + (z > 0).astype(jnp.int32) + (z < zs - 1).astype(jnp.int32)

    def tell(sem, peers):
        for there, peer in peers:
            if there is None:
                pl.semaphore_signal(sem, inc=1, device_id={"mesh": peer}, device_id_type=MESH)
            else:
                @pl.when(there)
                def _():
                    pl.semaphore_signal(sem, inc=1, device_id={"mesh": peer}, device_id_type=MESH)

    for k in range(chunks):
        local_copy(k, own, own_sem).start()
    barrier = pltpu.get_barrier_semaphore()
    crossing = jnp.logical_and(early, has_outer)
    tell(barrier, near + [(crossing, outer)])
    for k in range(chunks):
        local_copy(k, ext, ext_sem).start()
    ops_copy.start()

    for k in range(chunks):
        local_copy(k, own, own_sem).wait()
        for way, first in ((0, halo), (1, 0)):
            for h in range(halo):
                stage[k, way, h] = own[k][sends[0, first + h]]
        if k == 0:
            pl.semaphore_wait(barrier, near_count + crossing.astype(jnp.int32))
            tell(rounds.at[0], near)

        @pl.when(jnp.logical_and(early, k >= chunks - relayed))
        def _():
            relay_halo(k).start()

        @pl.when(jnp.logical_and(crossing, k < chunks - relayed))
        def _():
            outer_halo(k).start()

        if k == 0:
            @pl.when(late)
            def _():
                outer_halo(k).start()
        else:
            @pl.when(jnp.logical_and(late, relayed == 0))
            def _():
                outer_halo(k).start()
        pair_halo(k).start()

    @pl.when(jnp.logical_not(has_outer))
    def _():
        for k in range(chunks):
            ext[k][pl.ds(count + core * halo, halo)] = jnp.zeros((halo, size, width), jnp.bfloat16)

    pair_rows = 2 * size
    for k in range(chunks):
        def turn(r, carry):
            start = pl.multiple_of(r * pair_rows, pair_rows)
            turned[k * width:(k + 1) * width, pl.ds(start, pair_rows)] = (
                own[k][pl.ds(r * 2, 2)].reshape(pair_rows, width).T
            )
            return carry

        lax.fori_loop(0, count // 2, turn, 0)

    for r in range(zs):
        pl.semaphore_wait(rounds.at[r], near_count)
        if r + 1 < zs:
            tell(rounds.at[r + 1], near)

    ops_copy.wait()
    for k in range(chunks):
        local_copy(k, ext, ext_sem).wait()

    @pl.when(jnp.logical_and(late, relayed > 0))
    def _():
        pl.semaphore_wait(go, 1)
        for k in range(1, chunks):
            outer_halo(k).start()

    def serve(k):
        @pl.when(jnp.logical_and(early, k >= chunks - relaying))
        def _():
            relay_in(k).wait_recv()
            forward_halo(k).start()

        @pl.when(jnp.logical_and(early, k >= chunks - relayed))
        def _():
            relay_halo(k).wait_send()
            if k == last:
                pl.semaphore_signal(go, inc=1, device_id={"mesh": partner}, device_id_type=MESH)

    def relay_in(k):
        return remote(relay.at[k], relay.at[k], halo_send.at[k, 1], relay_recv.at[k], mate)

    def compute(k):
        pair_halo(k).wait_recv()

        @pl.when(has_outer)
        def _():
            forward_halo(k).wait_recv()

        def apply(g, carry):
            row = pl.multiple_of(g * size, size)
            diag = ext[k][g]
            for p in range(params):
                parts = [diag]
                for s in range(1, slots):
                    parts.append(ext[k][columns[p, s - 1, g]])
                left = jnp.concatenate([ops[p, g, s] for s in range(slots)], axis=1)
                made = jnp.dot(
                    left, jnp.concatenate(parts, axis=0), preferred_element_type=jnp.float32
                )
                image[pl.ds(row, size), p * width:(p + 1) * width] = made.astype(jnp.bfloat16)
            return carry

        lax.fori_loop(0, count, apply, 0, unroll=count)
        for h in range(2):
            made = jnp.dot(
                turned[h * half:(h + 1) * half, :], image[...], preferred_element_type=jnp.float32
            )
            part[k, h * half:(h + 1) * half] = made
            pair_out[k, h * half:(h + 1) * half] = made.astype(jnp.bfloat16)

            @pl.when(late if k < last else early)
            def _():
                pair_copy(k, h).start()

            if k == last:
                @pl.when(late)
                def _():
                    join(k, h)
                    far_start(k, range(h * n // 2, (h + 1) * n // 2))

    def join(k, h):
        pair_copy(k, h).wait_recv()
        rows = pl.ds(h * half, half)
        total = part[k, rows] + pair_in[k, rows].astype(jnp.float32)
        part[k, rows] = total
        z_out[k, rows] = total.astype(jnp.bfloat16)

    def far_start(k, devices):
        for d in devices:
            @pl.when(d != me)
            def _():
                far_copy(k, d).start()

    def gather(k):
        for h in range(2):
            join(k, h)
        if k < hops:
            for s in range(1, zs):
                z_copy(k, s).start()
        else:
            far_start(k, range(n))

    def across(k):
        total = part[k, pl.ds(pl.multiple_of(z * tall, tall), tall)]
        z_all(k).wait_recv()
        for s in range(1, zs):
            total = total + z_in[k, s - 1].astype(jnp.float32)
        x_own[k] = total
        x_out[k] = total.astype(jnp.bfloat16)
        for which in range(3):
            x_copy(k, which).start()

    def put(k, total):
        for p in range(params):
            out[:, p * basis_width + k * width:p * basis_width + (k + 1) * width] = total[
                :, p * width:(p + 1) * width
            ]

    def x_arrived(k, slot):
        remote(
            x_in.at[k, slot], x_in.at[k, slot], x_send.at[k], x_recv.at[k, slot], partner
        ).wait_recv()
        return x_in[k, slot].astype(jnp.float32)

    def finish_staged(k, mine):
        if mine:
            first = x_own[k, pl.ds(pl.multiple_of((x * CORES + core) * each, each), each)]
        else:
            first = x_arrived(k, 0)
        put(k, first + x_arrived(k, 1))

    def finish_far(k, mine):
        if mine:
            total = part[k, pl.ds(pl.multiple_of(me * each, each), each)]
        else:
            total = jnp.zeros((each, params * width), jnp.float32)
        came = chips - 1 if mine else chips
        remote(
            far_in.at[k - hops, pl.ds(0, came)], far_in.at[k - hops, pl.ds(0, came)],
            far_send.at[k - hops], far_recv.at[k - hops], partner,
        ).wait_recv()
        for s in range(came):
            total = total + far_in[k - hops, s].astype(jnp.float32)
        put(k, total)

    def finish(k, mine):
        if k < hops:
            finish_staged(k, mine)
        else:
            finish_far(k, mine)

    for k in range(min(SERVED, chunks)):
        serve(k)
    for k in range(chunks):
        if k + SERVED < chunks:
            serve(k + SERVED)
        compute(k)
        if k == last - 1:
            @pl.when(early)
            def _():
                gather(0)

    @pl.when(early)
    def _():
        for k in range(1, last):
            gather(k)
            if k - 1 < hops:
                across(k - 1)
        for k in range(last - 1, hops):
            across(k)
        for k in range(chunks):
            finish(k, k < last)

    @pl.when(late)
    def _():
        for k in range(chunks):
            finish(k, k == last)

    for k in range(chunks):
        pair_halo(k).wait_send()

        @pl.when(jnp.logical_or(late, jnp.logical_and(crossing, k < chunks - relayed)))
        def _():
            outer_halo(k).wait_send()

        @pl.when(jnp.logical_and(early, k >= chunks - relaying))
        def _():
            forward_halo(k).wait_send()

        @pl.when(late if k < last else early)
        def _():
            for h in range(2):
                pair_copy(k, h).wait_send()

        @pl.when(early if k < last else late)
        def _():
            if k < hops:
                z_all(k).wait_send()
                remote(
                    x_out.at[k, pl.ds(0, 3 * each)], x_out.at[k, pl.ds(0, 3 * each)],
                    x_send.at[k], x_recv.at[k, 0], partner,
                ).wait_send()
            else:
                rows = pl.ds(0, (n - 1) * each)
                remote(
                    z_out.at[k, rows], z_out.at[k, rows],
                    far_send.at[k - hops], far_recv.at[k - hops], partner,
                ).wait_send()


def relays_out(zs, chunks, z, x):
    if x == 1:
        return jnp.where(z < zs - 1, jnp.clip(chunks - z, 0, chunks), 0)
    return jnp.clip(z - 1, 0, chunks)


def fused_shards(n, basis, blocks, columns, sends):
    params, count, slots, size, _ = blocks.shape
    rows, basis_width = basis.shape
    halo = sends.shape[1] // 2
    zs = n // (CORES * XS)
    width = LANES
    chunks = basis_width // width
    each = basis_width // n
    tall = XS * CORES * each
    bf, f32 = jnp.bfloat16, jnp.float32
    wide = params * width
    dma = pltpu.SemaphoreType.DMA
    hops = chunks - 1 - FAR
    return pl.pallas_call(
        functools.partial(kernel, n, zs, width),
        out_shape=pltpu.VMEM((each, params * basis_width), f32),
        in_specs=[
            pl.BlockSpec(memory_space=pl.ANY),
            pl.BlockSpec(memory_space=pl.ANY),
            pl.BlockSpec(memory_space=pltpu.SMEM),
            pl.BlockSpec(memory_space=pltpu.SMEM),
        ],
        out_specs=pl.BlockSpec(memory_space=pltpu.VMEM),
        scratch_shapes=[pltpu.VMEM((count, size, width), bf) for _ in range(chunks)]
        + [pltpu.VMEM((count + 2 * halo, size, width), bf) for _ in range(chunks)]
        + [
            pltpu.VMEM((chunks, 2, halo, size, width), bf),
            pltpu.VMEM((chunks, halo, size, width), bf),
            pltpu.VMEM((basis_width, rows), bf),
            pltpu.VMEM(blocks.shape, bf),
            pltpu.VMEM((rows, wide), bf),
            pltpu.VMEM((chunks, basis_width, wide), f32),
            pltpu.VMEM((chunks, basis_width, wide), bf),
            pltpu.VMEM((chunks, basis_width, wide), bf),
            pltpu.VMEM((chunks, basis_width, wide), bf),
            pltpu.VMEM((hops, zs, tall, wide), bf),
            pltpu.VMEM((hops, tall, wide), f32),
            pltpu.VMEM((hops, tall, wide), bf),
            pltpu.VMEM((hops, 2, each, wide), bf),
            pltpu.VMEM((chunks - hops, n // CORES, each, wide), bf),
            dma((chunks,)),
            dma((chunks,)),
            dma,
            dma((chunks, 2)),
            dma((chunks, 2)),
            dma((chunks,)),
            dma((chunks,)),
            dma((chunks, 2)),
            dma((chunks, 2)),
            dma((hops,)),
            dma((hops,)),
            dma((hops,)),
            dma((hops, 2)),
            dma((chunks - hops,)),
            dma((chunks - hops,)),
            pltpu.SemaphoreType.REGULAR((zs,)),
            pltpu.SemaphoreType.REGULAR,
        ],
        compiler_params=pltpu.CompilerParams(collective_id=0, has_side_effects=True),
    )(basis.reshape(count, size, basis_width), blocks, jnp.swapaxes(columns, 1, 2), sends)


def solution(mesh):
    n = mesh.shape["mesh"]

    def shards(basis, blocks, columns, sends):
        each = basis.shape[1] // n
        tiled = basis.shape[1] % (n * 16) == 0 and LANES % max(each, 1) == 0
        chunked = basis.shape[1] // LANES > FAR + 1 and n % (XS * CORES) == 0
        if chunked and tiled and blocks.shape[3] == LANES:
            return fused_shards(n, basis, blocks, columns, sends)
        return plain_shards(basis, blocks, columns, sends)

    placed = (
        P(("grp", "mesh"), None),
        P(None, ("grp", "mesh"), None, None, None),
        P(None, ("grp", "mesh"), None),
        P(("grp", "mesh"), None),
    )
    return jax.shard_map(
        shards, mesh=mesh, in_specs=placed, out_specs=P(("grp", "mesh"), None), check_vma=False
    )
```

```python
import functools

import jax
import jax.numpy as jnp
from jax import lax
from jax.experimental import pallas as pl
from jax.experimental.pallas import tpu as pltpu
from jax.sharding import PartitionSpec as P

MESH = pl.DeviceIdType.MESH
CORES = 2
LANES = 128
XS = 2
FAR = 2
SERVED = 2
LAG = 1
GATED = 2


def from_behind(value, axis, steps):
    count = lax.axis_size(axis)
    leading, last = (max(0, -steps), min(count, count - steps))
    return lax.ppermute(value, axis, [(source, source + steps) for source in range(leading, last)])


def plain_shards(basis, blocks, columns, sends):
    count_params, count_blocks, count_slots, block_size, _ = blocks.shape
    basis_width = basis.shape[1]
    halo_count = sends.shape[1] // 2
    own_blocks = basis.reshape(count_blocks, block_size, basis_width)
    diag_index = jnp.arange(count_blocks, dtype=jnp.int32)[:, None]
    images = []
    upward = jnp.take(own_blocks, sends[0, halo_count:], axis=0)
    downward = jnp.take(own_blocks, sends[0, :halo_count], axis=0)
    from_below = from_behind(upward, "mesh", 1)
    from_above = from_behind(downward, "mesh", -1)
    extended = jnp.concatenate([own_blocks, from_below, from_above], axis=0)
    for param in range(count_params):
        slot_index = jnp.concatenate([diag_index, columns[param]], axis=1)
        gathered = jnp.take(extended, slot_index, axis=0)
        accumulated = jnp.einsum(
            "bsik,bskj->bij", blocks[param], gathered, preferred_element_type=jnp.float32
        )
        images.append(
            accumulated.astype(jnp.bfloat16).reshape(count_blocks * block_size, basis_width)
        )
    stacked_images = jnp.concatenate(images, axis=1)
    return lax.psum_scatter(
        lax.dot_general(
            basis, stacked_images, (((0,), (0,)), ((), ())), preferred_element_type=jnp.float32
        ),
        "mesh",
        scatter_dimension=0,
        tiled=True,
    )


def kernel(n, zs, width, basis, blocks, columns, sends, out, *scratch):
    chunks = basis.shape[2] // width
    own, scratch = scratch[:chunks], scratch[chunks:]
    ext, scratch = scratch[:chunks], scratch[chunks:]
    (
        stage, relay, turned, ops, image, part, pair_out, pair_in, z_out, z_in, x_own, x_out, x_in, far_in,
        own_sem, ext_sem, ops_sem, halo_send, halo_recv, relay_recv, forward_send,
        pair_send, pair_recv, z_send, z_recv, x_send, x_recv, far_send, far_recv, rounds, go,
    ) = scratch
    params, count, slots, size, _ = blocks.shape
    basis_width = basis.shape[2]
    halo = sends.shape[1] // 2
    half = basis_width // 2
    each = basis_width // n
    chips = n // CORES
    plane = XS * CORES
    tall = plane * each
    last = chunks - 1
    hops = chunks - FAR

    me = lax.axis_index("mesh")
    core = lax.rem(me, CORES)
    chip = me // CORES
    x = lax.rem(chip, XS)
    z = chip // XS
    early = core == x
    late = core != x

    def at(z, x, core):
        return (z * XS + x) * CORES + core

    partner = at(z, x, 1 - core)
    mate = at(z, 1 - x, 1 - core)
    outer = me - 1 + 2 * core
    has_outer = jnp.logical_and(outer >= 0, outer < n)
    onward = z + 1 - 2 * x
    relayed = (
        relays_out(zs, chunks, z, 1) * x + relays_out(zs, chunks, z, 0) * (1 - x)
    )
    relaying = (
        relays_out(zs, chunks, z, 0) * x + relays_out(zs, chunks, z, 1) * (1 - x)
    )

    def local_copy(k, buffers, sems):
        return pltpu.make_async_copy(
            basis.at[:, :, pl.ds(k * width, width)], buffers[k].at[pl.ds(0, count)], sems.at[k]
        )

    ops_copy = pltpu.make_async_copy(blocks, ops, ops_sem)

    def remote(source, target, sent, received, device):
        return pltpu.make_async_remote_copy(
            src_ref=source, dst_ref=target, send_sem=sent, recv_sem=received,
            device_id={"mesh": device}, device_id_type=MESH,
        )

    def pair_halo(k):
        return remote(
            stage.at[k, core], ext[k].at[pl.ds(count + core * halo, halo)],
            halo_send.at[k, 0], halo_recv.at[k, 0], partner,
        )

    def outer_halo(k):
        return remote(
            stage.at[k, 1 - core], ext[k].at[pl.ds(count + (1 - core) * halo, halo)],
            halo_send.at[k, 1], halo_recv.at[k, 1], outer,
        )

    def relay_halo(k):
        return remote(
            stage.at[k, 1 - core], relay.at[k], halo_send.at[k, 1], relay_recv.at[k], mate
        )

    def forward_halo(k):
        return remote(
            relay.at[k], ext[k].at[pl.ds(count + core * halo, halo)],
            forward_send.at[k], halo_recv.at[k, 1], at(onward, x, core),
        )

    def pair_copy(k, h):
        return remote(
            pair_out.at[k, pl.ds(h * half, half)], pair_in.at[k, pl.ds(h * half, half)],
            pair_send.at[k, h], pair_recv.at[k, h], partner,
        )

    def z_copy(k, step):
        target = lax.rem(z + step, zs)
        return remote(
            z_out.at[k, pl.ds(target * tall, tall)], z_in.at[k, step - 1],
            z_send.at[k], z_recv.at[k], at(target, x, core),
        )

    def z_all(k):
        came = z_in.at[k, pl.ds(0, zs - 1)]
        return remote(came, came, z_send.at[k], z_recv.at[k], partner)

    def x_copy(k, which):
        to_x = x if which == 2 else 1 - x
        to_core = core if which == 1 else 1 - core
        slot = 0 if which == 2 else 1
        return remote(
            x_out.at[k, pl.ds((to_x * CORES + to_core) * each, each)], x_in.at[k, slot],
            x_send.at[k], x_recv.at[k, slot], at(z, to_x, to_core),
        )

    def far_copy(k, d):
        slot = lax.rem(chip - d // CORES + 2 * chips - 1, chips)
        return remote(
            z_out.at[k, pl.ds(d * each, each)], far_in.at[k - hops, slot],
            far_send.at[k - hops], far_recv.at[k - hops], d,
        )

    near = [(None, partner), (None, mate), (z > 0, at(z - 1, x, core)), (z < zs - 1, at(z + 1, x, core))]
    near_count = 2 + (z > 0).astype(jnp.int32) + (z < zs - 1).astype(jnp.int32)

    def tell(sem, peers):
        for there, peer in peers:
            if there is None:
                pl.semaphore_signal(sem, inc=1, device_id={"mesh": peer}, device_id_type=MESH)
            else:
                @pl.when(there)
                def _():
                    pl.semaphore_signal(sem, inc=1, device_id={"mesh": peer}, device_id_type=MESH)

    for k in range(chunks):
        local_copy(k, own, own_sem).start()
    barrier = pltpu.get_barrier_semaphore()
    crossing = jnp.logical_and(early, has_outer)
    tell(barrier, near + [(crossing, outer)])
    for k in range(chunks):
        local_copy(k, ext, ext_sem).start()
    ops_copy.start()

    for k in range(chunks):
        local_copy(k, own, own_sem).wait()
        for way, first in ((0, halo), (1, 0)):
            for h in range(halo):
                stage[k, way, h] = own[k][sends[0, first + h]]
        if k == 0:
            pl.semaphore_wait(barrier, near_count + crossing.astype(jnp.int32))
            tell(rounds.at[0], near)

        @pl.when(jnp.logical_and(early, k >= chunks - relayed))
        def _():
            relay_halo(k).start()

        @pl.when(jnp.logical_and(crossing, k < chunks - relayed))
        def _():
            outer_halo(k).start()

        if k == 0:
            @pl.when(late)
            def _():
                outer_halo(k).start()
        else:
            @pl.when(jnp.logical_and(late, relayed < GATED))
            def _():
                outer_halo(k).start()
        pair_halo(k).start()

    @pl.when(jnp.logical_not(has_outer))
    def _():
        for k in range(chunks):
            ext[k][pl.ds(count + core * halo, halo)] = jnp.zeros((halo, size, width), jnp.bfloat16)

    pair_rows = 2 * size
    for k in range(chunks):
        def turn(r, carry):
            start = pl.multiple_of(r * pair_rows, pair_rows)
            turned[k * width:(k + 1) * width, pl.ds(start, pair_rows)] = (
                own[k][pl.ds(r * 2, 2)].reshape(pair_rows, width).T
            )
            return carry

        lax.fori_loop(0, count // 2, turn, 0)

    for r in range(zs):
        pl.semaphore_wait(rounds.at[r], near_count)
        if r + 1 < zs:
            tell(rounds.at[r + 1], near)

    ops_copy.wait()
    for k in range(chunks):
        local_copy(k, ext, ext_sem).wait()

    @pl.when(jnp.logical_and(late, relayed >= GATED))
    def _():
        pl.semaphore_wait(go, 1)
        for k in range(1, chunks):
            outer_halo(k).start()

    def serve(k):
        @pl.when(jnp.logical_and(early, k >= chunks - relayed))
        def _():
            relay_halo(k).wait_send()
            if k == last:
                @pl.when(relayed >= GATED)
                def _():
                    pl.semaphore_signal(
                        go, inc=1, device_id={"mesh": partner}, device_id_type=MESH
                    )

        @pl.when(jnp.logical_and(early, k >= chunks - relaying))
        def _():
            relay_in(k).wait_recv()
            forward_halo(k).start()

    def relay_in(k):
        return remote(relay.at[k], relay.at[k], halo_send.at[k, 1], relay_recv.at[k], mate)

    def compute(k):
        pair_halo(k).wait_recv()

        @pl.when(has_outer)
        def _():
            forward_halo(k).wait_recv()

        def apply(g, carry):
            row = pl.multiple_of(g * size, size)
            diag = ext[k][g]
            for p in range(params):
                parts = [diag]
                for s in range(1, slots):
                    parts.append(ext[k][columns[p, s - 1, g]])
                left = jnp.concatenate([ops[p, g, s] for s in range(slots)], axis=1)
                made = jnp.dot(
                    left, jnp.concatenate(parts, axis=0), preferred_element_type=jnp.float32
                )
                image[pl.ds(row, size), p * width:(p + 1) * width] = made.astype(jnp.bfloat16)
            return carry

        lax.fori_loop(0, count, apply, 0, unroll=count)
        for h in range(2):
            made = jnp.dot(
                turned[h * half:(h + 1) * half, :], image[...], preferred_element_type=jnp.float32
            )
            part[k, h * half:(h + 1) * half] = made
            pair_out[k, h * half:(h + 1) * half] = made.astype(jnp.bfloat16)

            @pl.when(late if k < hops else early)
            def _():
                pair_copy(k, h).start()

            if k >= hops:
                @pl.when(late)
                def _():
                    join(k, h)
                    far_start(k, range(h * n // 2, (h + 1) * n // 2))

    def join(k, h):
        pair_copy(k, h).wait_recv()
        rows = pl.ds(h * half, half)
        total = part[k, rows] + pair_in[k, rows].astype(jnp.float32)
        part[k, rows] = total
        z_out[k, rows] = total.astype(jnp.bfloat16)

    def far_start(k, devices):
        for d in devices:
            @pl.when(d != me)
            def _():
                far_copy(k, d).start()

    def gather(k):
        for h in range(2):
            join(k, h)
        for s in range(1, zs):
            z_copy(k, s).start()

    def across(k):
        total = part[k, pl.ds(pl.multiple_of(z * tall, tall), tall)]
        z_all(k).wait_recv()
        for s in range(1, zs):
            total = total + z_in[k, s - 1].astype(jnp.float32)
        x_own[k] = total
        x_out[k] = total.astype(jnp.bfloat16)
        for which in range(3):
            x_copy(k, which).start()

    def put(k, total):
        for p in range(params):
            out[:, p * basis_width + k * width:p * basis_width + (k + 1) * width] = total[
                :, p * width:(p + 1) * width
            ]

    def x_arrived(k, slot):
        remote(
            x_in.at[k, slot], x_in.at[k, slot], x_send.at[k], x_recv.at[k, slot], partner
        ).wait_recv()
        return x_in[k, slot].astype(jnp.float32)

    def finish_staged(k, mine):
        if mine:
            first = x_own[k, pl.ds(pl.multiple_of((x * CORES + core) * each, each), each)]
        else:
            first = x_arrived(k, 0)
        put(k, first + x_arrived(k, 1))

    def finish_far(k, mine):
        if mine:
            total = part[k, pl.ds(pl.multiple_of(me * each, each), each)]
        else:
            total = jnp.zeros((each, params * width), jnp.float32)
        came = chips - 1 if mine else chips
        remote(
            far_in.at[k - hops, pl.ds(0, came)], far_in.at[k - hops, pl.ds(0, came)],
            far_send.at[k - hops], far_recv.at[k - hops], partner,
        ).wait_recv()
        for s in range(came):
            total = total + far_in[k - hops, s].astype(jnp.float32)
        put(k, total)

    def finish(k, mine):
        if k < hops:
            finish_staged(k, mine)
        else:
            finish_far(k, mine)

    for k in range(min(SERVED, chunks)):
        serve(k)
    for k in range(chunks):
        if k + SERVED < chunks:
            serve(k + SERVED)
        compute(k)
        if 0 <= k - LAG < hops:
            @pl.when(early)
            def _():
                gather(k - LAG)

    @pl.when(early)
    def _():
        for k in range(max(chunks - LAG, 0), hops):
            gather(k)
        for k in range(hops):
            across(k)
        for k in range(chunks):
            finish(k, k < hops)

    @pl.when(late)
    def _():
        for k in range(chunks):
            finish(k, k >= hops)

    for k in range(chunks):
        pair_halo(k).wait_send()

        @pl.when(jnp.logical_or(late, jnp.logical_and(crossing, k < chunks - relayed)))
        def _():
            outer_halo(k).wait_send()

        @pl.when(jnp.logical_and(early, k >= chunks - relaying))
        def _():
            forward_halo(k).wait_send()

        @pl.when(late if k < hops else early)
        def _():
            for h in range(2):
                pair_copy(k, h).wait_send()

        @pl.when(early if k < hops else late)
        def _():
            if k < hops:
                z_all(k).wait_send()
                remote(
                    x_out.at[k, pl.ds(0, 3 * each)], x_out.at[k, pl.ds(0, 3 * each)],
                    x_send.at[k], x_recv.at[k, 0], partner,
                ).wait_send()
            else:
                rows = pl.ds(0, (n - 1) * each)
                remote(
                    z_out.at[k, rows], z_out.at[k, rows],
                    far_send.at[k - hops], far_recv.at[k - hops], partner,
                ).wait_send()


def relays_out(zs, chunks, z, x):
    if x == 1:
        return jnp.where(z < zs - 1, jnp.clip(chunks - 1 - z, 0, chunks), 0)
    return jnp.clip(z - 1, 0, chunks)


def fused_shards(n, basis, blocks, columns, sends):
    params, count, slots, size, _ = blocks.shape
    rows, basis_width = basis.shape
    halo = sends.shape[1] // 2
    zs = n // (CORES * XS)
    width = LANES
    chunks = basis_width // width
    each = basis_width // n
    tall = XS * CORES * each
    bf, f32 = jnp.bfloat16, jnp.float32
    wide = params * width
    dma = pltpu.SemaphoreType.DMA
    hops = chunks - FAR
    return pl.pallas_call(
        functools.partial(kernel, n, zs, width),
        out_shape=pltpu.VMEM((each, params * basis_width), f32),
        in_specs=[
            pl.BlockSpec(memory_space=pl.ANY),
            pl.BlockSpec(memory_space=pl.ANY),
            pl.BlockSpec(memory_space=pltpu.SMEM),
            pl.BlockSpec(memory_space=pltpu.SMEM),
        ],
        out_specs=pl.BlockSpec(memory_space=pltpu.VMEM),
        scratch_shapes=[pltpu.VMEM((count, size, width), bf) for _ in range(chunks)]
        + [pltpu.VMEM((count + 2 * halo, size, width), bf) for _ in range(chunks)]
        + [
            pltpu.VMEM((chunks, 2, halo, size, width), bf),
            pltpu.VMEM((chunks, halo, size, width), bf),
            pltpu.VMEM((basis_width, rows), bf),
            pltpu.VMEM(blocks.shape, bf),
            pltpu.VMEM((rows, wide), bf),
            pltpu.VMEM((chunks, basis_width, wide), f32),
            pltpu.VMEM((chunks, basis_width, wide), bf),
            pltpu.VMEM((chunks, basis_width, wide), bf),
            pltpu.VMEM((chunks, basis_width, wide), bf),
            pltpu.VMEM((hops, zs, tall, wide), bf),
            pltpu.VMEM((hops, tall, wide), f32),
            pltpu.VMEM((hops, tall, wide), bf),
            pltpu.VMEM((hops, 2, each, wide), bf),
            pltpu.VMEM((chunks - hops, n // CORES, each, wide), bf),
            dma((chunks,)),
            dma((chunks,)),
            dma,
            dma((chunks, 2)),
            dma((chunks, 2)),
            dma((chunks,)),
            dma((chunks,)),
            dma((chunks, 2)),
            dma((chunks, 2)),
            dma((hops,)),
            dma((hops,)),
            dma((hops,)),
            dma((hops, 2)),
            dma((chunks - hops,)),
            dma((chunks - hops,)),
            pltpu.SemaphoreType.REGULAR((zs,)),
            pltpu.SemaphoreType.REGULAR,
        ],
        compiler_params=pltpu.CompilerParams(collective_id=0, has_side_effects=True),
    )(basis.reshape(count, size, basis_width), blocks, jnp.swapaxes(columns, 1, 2), sends)


def solution(mesh):
    n = mesh.shape["mesh"]

    def shards(basis, blocks, columns, sends):
        each = basis.shape[1] // n
        tiled = basis.shape[1] % (n * 16) == 0 and LANES % max(each, 1) == 0
        chunked = basis.shape[1] // LANES > FAR and n % (XS * CORES) == 0
        if chunked and tiled and blocks.shape[3] == LANES:
            return fused_shards(n, basis, blocks, columns, sends)
        return plain_shards(basis, blocks, columns, sends)

    placed = (
        P(("grp", "mesh"), None),
        P(None, ("grp", "mesh"), None, None, None),
        P(None, ("grp", "mesh"), None),
        P(("grp", "mesh"), None),
    )
    return jax.shard_map(
        shards, mesh=mesh, in_specs=placed, out_specs=P(("grp", "mesh"), None), check_vma=False
    )
```

```python
import functools

import jax
import jax.numpy as jnp
from jax import lax
from jax.experimental import pallas as pl
from jax.experimental.pallas import tpu as pltpu
from jax.sharding import PartitionSpec as P

MESH = pl.DeviceIdType.MESH
CORES = 2
LANES = 128
XS = 2
EARLY = 1
FAR = 2
SERVED = 2
LAG = 1
SLACK = 2
HOP = 2
AHEAD = 3
CLOSE = 3
GATED = 2


def from_behind(value, axis, steps):
    count = lax.axis_size(axis)
    leading, last = (max(0, -steps), min(count, count - steps))
    return lax.ppermute(value, axis, [(source, source + steps) for source in range(leading, last)])


def plain_shards(basis, blocks, columns, sends):
    count_params, count_blocks, count_slots, block_size, _ = blocks.shape
    basis_width = basis.shape[1]
    halo_count = sends.shape[1] // 2
    own_blocks = basis.reshape(count_blocks, block_size, basis_width)
    diag_index = jnp.arange(count_blocks, dtype=jnp.int32)[:, None]
    images = []
    upward = jnp.take(own_blocks, sends[0, halo_count:], axis=0)
    downward = jnp.take(own_blocks, sends[0, :halo_count], axis=0)
    from_below = from_behind(upward, "mesh", 1)
    from_above = from_behind(downward, "mesh", -1)
    extended = jnp.concatenate([own_blocks, from_below, from_above], axis=0)
    for param in range(count_params):
        slot_index = jnp.concatenate([diag_index, columns[param]], axis=1)
        gathered = jnp.take(extended, slot_index, axis=0)
        accumulated = jnp.einsum(
            "bsik,bskj->bij", blocks[param], gathered, preferred_element_type=jnp.float32
        )
        images.append(
            accumulated.astype(jnp.bfloat16).reshape(count_blocks * block_size, basis_width)
        )
    stacked_images = jnp.concatenate(images, axis=1)
    return lax.psum_scatter(
        lax.dot_general(
            basis, stacked_images, (((0,), (0,)), ((), ())), preferred_element_type=jnp.float32
        ),
        "mesh",
        scatter_dimension=0,
        tiled=True,
    )


def kernel(n, zs, width, basis, blocks, columns, sends, out, *scratch):
    chunks = basis.shape[2] // width
    own, scratch = scratch[:chunks], scratch[chunks:]
    ext, scratch = scratch[:chunks], scratch[chunks:]
    (
        stage, relay, turned, ops, diagonal, image, part, pair_out, pair_in, z_out, z_in, x_own, x_out, x_in,
        far_in, own_sem, ops_sem, halo_send, halo_recv, relay_recv, forward_send,
        pair_send, pair_recv, z_send, z_recv, x_send, x_recv, far_send, far_recv, rounds, go,
    ) = scratch
    params, count, slots, size, _ = blocks.shape
    basis_width = basis.shape[2]
    halo = sends.shape[1] // 2
    half = basis_width // 2
    each = basis_width // n
    chips = n // CORES
    plane = XS * CORES
    tall = plane * each
    last = chunks - 1
    hops = chunks - FAR
    steps = zs.bit_length() - 1

    me = lax.axis_index("mesh")
    core = lax.rem(me, CORES)
    chip = me // CORES
    x = lax.rem(chip, XS)
    z = chip // XS
    early = core == x
    late = core != x

    def at(z, x, core):
        return (z * XS + x) * CORES + core

    partner = at(z, x, 1 - core)
    mate = at(z, 1 - x, 1 - core)
    outer = me - 1 + 2 * core
    has_outer = jnp.logical_and(outer >= 0, outer < n)
    onward = z + 1 - 2 * x
    relayed = (
        relays_out(zs, chunks, z, 1) * x + relays_out(zs, chunks, z, 0) * (1 - x)
    )
    relaying = (
        relays_out(zs, chunks, z, 0) * x + relays_out(zs, chunks, z, 1) * (1 - x)
    )

    def local_copy(k, buffers, sems):
        return pltpu.make_async_copy(
            basis.at[:, :, pl.ds(k * width, width)], buffers[k].at[pl.ds(0, count)], sems.at[k]
        )

    ops_copy = pltpu.make_async_copy(blocks, ops, ops_sem)

    def remote(source, target, sent, received, device):
        return pltpu.make_async_remote_copy(
            src_ref=source, dst_ref=target, send_sem=sent, recv_sem=received,
            device_id={"mesh": device}, device_id_type=MESH,
        )

    def pair_halo(k):
        return remote(
            stage.at[k, core], ext[k].at[pl.ds(count + core * halo, halo)],
            halo_send.at[0], halo_recv.at[chunks], partner,
        )

    def outer_halo(k):
        return remote(
            stage.at[k, 1 - core], ext[k].at[pl.ds(count + (1 - core) * halo, halo)],
            halo_send.at[1], halo_recv.at[k], outer,
        )

    def relay_halo(k):
        return remote(
            stage.at[k, 1 - core], relay.at[k], halo_send.at[2], relay_recv.at[k], mate
        )

    def forward_halo(k):
        return remote(
            relay.at[k], ext[k].at[pl.ds(count + core * halo, halo)],
            forward_send, halo_recv.at[k], at(onward, x, core),
        )

    def half_rows(i):
        return pl.ds(i * half, half)

    def pair_copy(k):
        return remote(pair_out.at[k], pair_in.at[k], pair_send, pair_recv.at[k], partner)

    def blocks_sent(count, sent):
        moved = stage.at[pl.ds(0, count), 0]
        return remote(moved, moved, sent, halo_recv.at[0], partner)

    def turn_of(k):
        return k if k < EARLY else k - EARLY

    def halving(k, b):
        stride = 2 ** b
        low, bit = lax.rem(z, stride), lax.rem(z // stride, 2)
        kept = [low + bit * stride + j * 2 * stride for j in range(zs // (2 * stride))]
        given = [low + (1 - bit) * stride + j * 2 * stride for j in range(zs // (2 * stride))]
        return kept, given, z + (1 - 2 * bit) * stride, zs - zs // stride

    def tall_rows(t):
        return pl.ds(pl.multiple_of(t * tall, tall), tall)

    def halve_start(k, b):
        _, given, there, slot = halving(k, b)
        for j, t in enumerate(given):
            remote(
                z_out.at[k, tall_rows(t)], z_in.at[k, slot + j],
                z_send.at[turn_of(k)], z_recv.at[turn_of(k), b], at(there, x, core),
            ).start()

    def halve_add(k, b):
        kept, _, _, slot = halving(k, b)
        came = z_in.at[k, pl.ds(slot, len(kept))]
        remote(came, came, z_send.at[turn_of(k)], z_recv.at[turn_of(k), b], partner).wait_recv()
        for j, t in enumerate(kept):
            total = part[k, tall_rows(t)] + z_in[k, slot + j].astype(jnp.float32)
            part[k, tall_rows(t)] = total
            z_out[k, tall_rows(t)] = total.astype(jnp.bfloat16)

    def z_start(k, j):
        target = j
        slot = lax.rem(z - target + 2 * zs - 1, zs)

        @pl.when(target != z)
        def _():
            remote(
                z_out.at[k, pl.ds(target * tall, tall)], z_in.at[k, slot],
                z_send.at[turn_of(k)], z_recv.at[turn_of(k), 0], at(target, x, core),
            ).start()

    def z_all(k):
        came = z_in.at[k, pl.ds(0, zs - 1)]
        return remote(came, came, z_send.at[turn_of(k)], z_recv.at[turn_of(k), 0], partner)

    def x_copy(k, which):
        to_x = x if which == 2 else 1 - x
        to_core = core if which == 1 else 1 - core
        slot = 0 if which == 2 else 1
        return remote(
            x_out.at[k, pl.ds(pl.multiple_of((to_x * CORES + to_core) * each, each), each)], x_in.at[k, slot],
            x_send.at[turn_of(k)], x_recv.at[k], at(z, to_x, to_core),
        )

    def far_start(k, i):
        for j in range(zs // 2):
            to_z = i * (zs // 2) + j
            for to_x in range(XS):
                slot = lax.rem(chip - to_z * XS - to_x + 2 * chips - 1, chips)
                for to_core in range(CORES):
                    owner = at(to_z, to_x, to_core)

                    @pl.when(owner != me)
                    def _():
                        remote(
                            z_out.at[k, pl.ds(owner * each, each)],
                            far_in.at[k - hops, slot], far_send,
                            far_recv.at[k - hops], owner,
                        ).start()

    near = [(None, partner), (None, mate), (z > 0, at(z - 1, x, core)), (z < zs - 1, at(z + 1, x, core))]
    near_count = 2 + (z > 0).astype(jnp.int32) + (z < zs - 1).astype(jnp.int32)

    crossing = jnp.logical_and(early, has_outer)
    close = near[:2] + [(crossing, outer)]
    close_count = 2 + crossing.astype(jnp.int32)

    def tell(sem, peers):
        for there, peer in peers:
            if there is None:
                pl.semaphore_signal(sem, inc=1, device_id={"mesh": peer}, device_id_type=MESH)
            else:
                @pl.when(there)
                def _():
                    pl.semaphore_signal(sem, inc=1, device_id={"mesh": peer}, device_id_type=MESH)

    for k in range(chunks):
        local_copy(k, own, own_sem).start()
    barrier = pltpu.get_barrier_semaphore()
    tell(barrier, close)
    ops_copy.start()

    for k in range(chunks):
        local_copy(k, own, own_sem).wait()
        local_copy(k, ext, own_sem).start()
        for way, first in ((0, halo), (1, 0)):
            for h in range(halo):
                stage[k, way, h] = own[k][sends[0, first + h]]
        if k == 0:
            pl.semaphore_wait(barrier, close_count)
            tell(rounds.at[0], close)

        @pl.when(jnp.logical_and(early, k >= chunks - relayed))
        def _():
            relay_halo(k).start()

        @pl.when(jnp.logical_and(crossing, k < jnp.minimum(chunks - relayed, AHEAD)))
        def _():
            outer_halo(k).start()

        if k == 0:
            @pl.when(late)
            def _():
                outer_halo(k).start()
        else:
            @pl.when(jnp.logical_and(late, relayed < GATED))
            def _():
                outer_halo(k).start()
        pair_halo(k).start()

    @pl.when(jnp.logical_not(has_outer))
    def _():
        for k in range(chunks):
            ext[k][pl.ds(count + core * halo, halo)] = jnp.zeros((halo, size, width), jnp.bfloat16)

    pair_rows = 2 * size
    for k in range(chunks):
        def turn(r, carry):
            start = pl.multiple_of(r * pair_rows, pair_rows)
            turned[k * width:(k + 1) * width, pl.ds(start, pair_rows)] = (
                own[k][pl.ds(r * 2, 2)].reshape(pair_rows, width).T
            )
            return carry

        lax.fori_loop(0, count // 2, turn, 0)

    for r in range(zs + 1):
        pl.semaphore_wait(rounds.at[r], close_count if r < CLOSE else near_count)
        if r < zs:
            tell(rounds.at[r + 1], close if r + 1 < CLOSE else near)

    ops_copy.wait()
    for k in range(chunks):
        local_copy(k, ext, own_sem).wait()

    def precompute(g, carry):
        row = pl.multiple_of(g * size, size)
        for p in range(params):
            diagonal[pl.ds(row, size), p * width:(p + 1) * width] = jnp.dot(
                ops[p, g, 0], own[last][g], preferred_element_type=jnp.float32
            )
        return carry

    lax.fori_loop(0, count, precompute, 0, unroll=2)

    @pl.when(jnp.logical_and(late, relayed >= GATED))
    def _():
        pl.semaphore_wait(go, 1)
        for k in range(1, chunks):
            outer_halo(k).start()

    def serve(k):
        if k == last:
            for c in range(1, chunks + 1):
                @pl.when(jnp.logical_and(early, relayed == c))
                def _():
                    blocks_sent(c, halo_send.at[2]).wait_send()
                    if c >= GATED:
                        pl.semaphore_signal(
                            go, inc=1, device_id={"mesh": partner}, device_id_type=MESH
                        )

        @pl.when(jnp.logical_and(early, k >= chunks - relaying))
        def _():
            relay_in(k).wait_recv()
            forward_halo(k).start()

    def relay_in(k):
        return remote(relay.at[k], relay.at[k], halo_send.at[2], relay_recv.at[k], mate)

    def compute(k):
        if k == 0:
            both = stage.at[:, core]
            remote(both, both, halo_send.at[0], halo_recv.at[chunks], partner).wait_recv()

        @pl.when(has_outer)
        def _():
            forward_halo(k).wait_recv()

        def apply(g, carry):
            row = pl.multiple_of(g * size, size)
            first = 1 if k == last else 0
            diag = [] if k == last else [ext[k][g]]
            for p in range(params):
                parts = list(diag)
                for s in range(1, slots):
                    parts.append(ext[k][columns[p, s - 1, g]])
                left = jnp.concatenate([ops[p, g, s] for s in range(first, slots)], axis=1)
                made = jnp.dot(
                    left, jnp.concatenate(parts, axis=0), preferred_element_type=jnp.float32
                )
                if k == last:
                    made = made + diagonal[pl.ds(row, size), p * width:(p + 1) * width]
                image[pl.ds(row, size), p * width:(p + 1) * width] = made.astype(jnp.bfloat16)
            return carry

        lax.fori_loop(0, count, apply, 0, unroll=count)
        for i in range(2):
            made = jnp.dot(
                turned[half_rows(i), :], image[...], preferred_element_type=jnp.float32
            )
            part[k, half_rows(i)] = made
            pair_out[k, half_rows(i)] = made.astype(jnp.bfloat16)

            if i == 1:
                @pl.when(late if k < EARLY else early)
                def _():
                    pair_copy(k).start()

            if k >= EARLY:
                @pl.when(late)
                def _():
                    join(k, i)
                    if k < hops:
                        z_start_half(k, i)
                    else:
                        far_start(k, i)

    def join(k, i):
        if i == 0:
            pair_copy(k).wait_recv()
        rows = half_rows(i)
        total = part[k, rows] + pair_in[k, rows].astype(jnp.float32)
        part[k, rows] = total
        z_out[k, rows] = total.astype(jnp.bfloat16)

    def z_start_half(k, i):
        if i == 0:
            for j in range(zs // 2):
                z_start(k, j)
        else:
            for j in range(zs // 2, zs):
                z_start(k, j)

    def gather(k):
        for i in range(2):
            join(k, i)
        halve_start(k, 0)

    def hop(k):
        for b in range(1, steps):
            halve_add(k, b - 1)
            halve_start(k, b)

    def across(k):
        if k < EARLY:
            halve_add(k, steps - 1)
            total = part[k, tall_rows(z)]
        else:
            total = part[k, tall_rows(z)]
            z_all(k).wait_recv()
            for s in range(1, zs):
                total = total + z_in[k, s - 1].astype(jnp.float32)
        x_own[k] = total
        x_out[k] = total.astype(jnp.bfloat16)
        for which in range(3):
            x_copy(k, which).start()

    def put(k, total):
        for p in range(params):
            out[:, p * basis_width + k * width:p * basis_width + (k + 1) * width] = total[
                :, p * width:(p + 1) * width
            ]

    def finish_staged(k, mine):
        came = x_in.at[k, pl.ds(1 if mine else 0, 1 if mine else 2)]
        remote(came, came, x_send.at[0], x_recv.at[k], partner).wait_recv()
        if mine:
            first = x_own[k, pl.ds(pl.multiple_of((x * CORES + core) * each, each), each)]
        else:
            first = x_in[k, 0].astype(jnp.float32)
        put(k, first + x_in[k, 1].astype(jnp.float32))

    def finish_far(k, mine):
        if mine:
            total = part[k, pl.ds(pl.multiple_of(me * each, each), each)]
        else:
            total = jnp.zeros((each, params * width), jnp.float32)
        came = chips - 1 if mine else chips
        remote(
            far_in.at[k - hops, pl.ds(0, came)], far_in.at[k - hops, pl.ds(0, came)],
            far_send, far_recv.at[k - hops], partner,
        ).wait_recv()
        for s in range(came):
            total = total + far_in[k - hops, s].astype(jnp.float32)
        put(k, total)

    def finish(k, mine):
        if k < hops:
            finish_staged(k, mine)
        else:
            finish_far(k, mine)

    for k in range(min(SERVED, chunks)):
        serve(k)
    for k in range(chunks):
        if k + SERVED < chunks:
            serve(k + SERVED)
        compute(k)
        if k + AHEAD < chunks:
            @pl.when(jnp.logical_and(crossing, k + AHEAD < chunks - relayed))
            def _():
                outer_halo(k + AHEAD).start()
        if 0 <= k - LAG < EARLY:
            @pl.when(early)
            def _():
                gather(k - LAG)
        if 0 <= k - HOP < EARLY:
            @pl.when(early)
            def _():
                hop(k - HOP)
        if EARLY <= k - SLACK < hops:
            @pl.when(late)
            def _():
                across(k - SLACK)

    @pl.when(early)
    def _():
        for k in range(EARLY):
            across(k)
        for k in range(chunks):
            finish(k, k < EARLY)

    @pl.when(late)
    def _():
        for k in range(chunks):
            finish(k, k >= EARLY)

    blocks_sent(chunks, halo_send.at[0]).wait_send()

    @pl.when(late)
    def _():
        blocks_sent(chunks, halo_send.at[1]).wait_send()

    for c in range(1, chunks + 1):
        @pl.when(jnp.logical_and(crossing, relayed == chunks - c))
        def _():
            blocks_sent(c, halo_send.at[1]).wait_send()

        @pl.when(jnp.logical_and(early, relaying == c))
        def _():
            blocks_sent(c, forward_send).wait_send()

    def sums_sent(first, end):
        summed = pair_out.at[pl.ds(first, end - first)]
        remote(summed, summed, pair_send, pair_recv.at[0], partner).wait_send()

    def staged_sent(k):
        z_all(k).wait_send()
        rows = x_out.at[k, pl.ds(0, 3 * each)]
        remote(rows, rows, x_send.at[turn_of(k)], x_recv.at[k], partner).wait_send()

    @pl.when(early)
    def _():
        sums_sent(EARLY, chunks)
        for k in range(EARLY):
            staged_sent(k)

    @pl.when(late)
    def _():
        sums_sent(0, EARLY)
        for k in range(EARLY, hops):
            staged_sent(k)
        rows = z_out.at[pl.ds(hops, chunks - hops), pl.ds(0, (n - 1) * each)]
        remote(rows, rows, far_send, far_recv.at[0], partner).wait_send()


def relays_out(zs, chunks, z, x):
    if x == 1:
        return jnp.where(z < zs - 1, jnp.clip(chunks - 1 - z, 0, chunks), 0)
    return jnp.clip(z - 1, 0, chunks)


def fused_shards(n, basis, blocks, columns, sends):
    params, count, slots, size, _ = blocks.shape
    rows, basis_width = basis.shape
    halo = sends.shape[1] // 2
    zs = n // (CORES * XS)
    width = LANES
    chunks = basis_width // width
    each = basis_width // n
    tall = XS * CORES * each
    bf, f32 = jnp.bfloat16, jnp.float32
    wide = params * width
    dma = pltpu.SemaphoreType.DMA
    hops = chunks - FAR
    turns = max(EARLY, hops - EARLY)
    return pl.pallas_call(
        functools.partial(kernel, n, zs, width),
        out_shape=pltpu.VMEM((each, params * basis_width), f32),
        in_specs=[
            pl.BlockSpec(memory_space=pl.ANY),
            pl.BlockSpec(memory_space=pl.ANY),
            pl.BlockSpec(memory_space=pltpu.SMEM),
            pl.BlockSpec(memory_space=pltpu.SMEM),
        ],
        out_specs=pl.BlockSpec(memory_space=pltpu.VMEM),
        scratch_shapes=[pltpu.VMEM((count, size, width), bf) for _ in range(chunks)]
        + [pltpu.VMEM((count + 2 * halo, size, width), bf) for _ in range(chunks)]
        + [
            pltpu.VMEM((chunks, 2, halo, size, width), bf),
            pltpu.VMEM((chunks, halo, size, width), bf),
            pltpu.VMEM((basis_width, rows), bf),
            pltpu.VMEM(blocks.shape, bf),
            pltpu.VMEM((rows, wide), f32),
            pltpu.VMEM((rows, wide), bf),
            pltpu.VMEM((chunks, basis_width, wide), f32),
            pltpu.VMEM((chunks, basis_width, wide), bf),
            pltpu.VMEM((chunks, basis_width, wide), bf),
            pltpu.VMEM((chunks, basis_width, wide), bf),
            pltpu.VMEM((hops, zs, tall, wide), bf),
            pltpu.VMEM((hops, tall, wide), f32),
            pltpu.VMEM((hops, tall, wide), bf),
            pltpu.VMEM((hops, 2, each, wide), bf),
            pltpu.VMEM((chunks - hops, n // CORES, each, wide), bf),
            dma((chunks,)),
            dma,
            dma((3,)),
            dma((chunks + 1,)),
            dma((chunks,)),
            dma,
            dma,
            dma((chunks,)),
            dma((turns,)),
            dma((turns, zs.bit_length() - 1)),
            dma((turns,)),
            dma((hops,)),
            dma,
            dma((chunks - hops,)),
            pltpu.SemaphoreType.REGULAR((zs + 1,)),
            pltpu.SemaphoreType.REGULAR,
        ],
        compiler_params=pltpu.CompilerParams(collective_id=0, has_side_effects=True),
    )(basis.reshape(count, size, basis_width), blocks, jnp.swapaxes(columns, 1, 2), sends)


def solution(mesh):
    n = mesh.shape["mesh"]

    def shards(basis, blocks, columns, sends):
        each = basis.shape[1] // n
        tiled = basis.shape[1] % (n * 16) == 0 and LANES % max(each, 1) == 0
        chunked = basis.shape[1] // LANES >= EARLY + FAR and n // (XS * CORES) in (2, 4, 8)
        if chunked and tiled and blocks.shape[3] == LANES:
            return fused_shards(n, basis, blocks, columns, sends)
        return plain_shards(basis, blocks, columns, sends)

    placed = (
        P(("grp", "mesh"), None),
        P(None, ("grp", "mesh"), None, None, None),
        P(None, ("grp", "mesh"), None),
        P(("grp", "mesh"), None),
    )
    return jax.shard_map(
        shards, mesh=mesh, in_specs=placed, out_specs=P(("grp", "mesh"), None), check_vma=False
    )
```

```python
import functools

import jax
import jax.numpy as jnp
from jax import lax
from jax.experimental import pallas as pl
from jax.experimental.pallas import tpu as pltpu
from jax.sharding import PartitionSpec as P

MESH = pl.DeviceIdType.MESH
CORES = 2
LANES = 128
XS = 2
EARLY = 1
FAR = 2
SERVED = 2
LAG = 0
DIRECT = ((), (0,), (1, 2, 3))
SLACK = 2
CLOSE = 3
GATED = 2


def from_behind(value, axis, steps):
    count = lax.axis_size(axis)
    leading, last = (max(0, -steps), min(count, count - steps))
    return lax.ppermute(value, axis, [(source, source + steps) for source in range(leading, last)])


def plain_shards(basis, blocks, columns, sends):
    count_params, count_blocks, count_slots, block_size, _ = blocks.shape
    basis_width = basis.shape[1]
    halo_count = sends.shape[1] // 2
    own_blocks = basis.reshape(count_blocks, block_size, basis_width)
    diag_index = jnp.arange(count_blocks, dtype=jnp.int32)[:, None]
    images = []
    upward = jnp.take(own_blocks, sends[0, halo_count:], axis=0)
    downward = jnp.take(own_blocks, sends[0, :halo_count], axis=0)
    from_below = from_behind(upward, "mesh", 1)
    from_above = from_behind(downward, "mesh", -1)
    extended = jnp.concatenate([own_blocks, from_below, from_above], axis=0)
    for param in range(count_params):
        slot_index = jnp.concatenate([diag_index, columns[param]], axis=1)
        gathered = jnp.take(extended, slot_index, axis=0)
        accumulated = jnp.einsum(
            "bsik,bskj->bij", blocks[param], gathered, preferred_element_type=jnp.float32
        )
        images.append(
            accumulated.astype(jnp.bfloat16).reshape(count_blocks * block_size, basis_width)
        )
    stacked_images = jnp.concatenate(images, axis=1)
    return lax.psum_scatter(
        lax.dot_general(
            basis, stacked_images, (((0,), (0,)), ((), ())), preferred_element_type=jnp.float32
        ),
        "mesh",
        scatter_dimension=0,
        tiled=True,
    )


def kernel(n, zs, width, basis, blocks, columns, sends, out, *scratch):
    chunks = basis.shape[2] // width
    own, scratch = scratch[:chunks], scratch[chunks:]
    ext, scratch = scratch[:chunks], scratch[chunks:]
    (
        stage, relay, turned, ops, diagonal, image, part, pair_out, pair_in, z_out, z_in, x_own, x_out, x_in,
        far_in, own_sem, ops_sem, halo_send, halo_recv, relay_recv, forward_send,
        pair_send, pair_recv, z_send, z_recv, x_send, x_recv, far_send, far_recv, rounds, go,
    ) = scratch
    params, count, slots, size, _ = blocks.shape
    basis_width = basis.shape[2]
    halo = sends.shape[1] // 2
    half = basis_width // 2
    each = basis_width // n
    chips = n // CORES
    plane = XS * CORES
    tall = plane * each
    last = chunks - 1
    hops = chunks - FAR

    me = lax.axis_index("mesh")
    core = lax.rem(me, CORES)
    chip = me // CORES
    x = lax.rem(chip, XS)
    z = chip // XS
    early = core == x
    late = core != x

    def at(z, x, core):
        return (z * XS + x) * CORES + core

    partner = at(z, x, 1 - core)
    mate = at(z, 1 - x, 1 - core)
    outer = me - 1 + 2 * core
    has_outer = jnp.logical_and(outer >= 0, outer < n)
    onward = z + 1 - 2 * x
    relayed = (
        relays_out(zs, chunks, z, 1) * x + relays_out(zs, chunks, z, 0) * (1 - x)
    )
    relaying = (
        relays_out(zs, chunks, z, 0) * x + relays_out(zs, chunks, z, 1) * (1 - x)
    )

    def local_copy(k, buffers, sems):
        return pltpu.make_async_copy(
            basis.at[:, :, pl.ds(k * width, width)], buffers[k].at[pl.ds(0, count)], sems.at[k]
        )

    ops_copy = pltpu.make_async_copy(blocks, ops, ops_sem)

    def remote(source, target, sent, received, device):
        return pltpu.make_async_remote_copy(
            src_ref=source, dst_ref=target, send_sem=sent, recv_sem=received,
            device_id={"mesh": device}, device_id_type=MESH,
        )

    def pair_halo(k):
        return remote(
            stage.at[k, core], ext[k].at[pl.ds(count + core * halo, halo)],
            halo_send.at[0], halo_recv.at[chunks], partner,
        )

    def outer_halo(k):
        return remote(
            stage.at[k, 1 - core], ext[k].at[pl.ds(count + (1 - core) * halo, halo)],
            halo_send.at[1], halo_recv.at[k], outer,
        )

    def relay_halo(k):
        return remote(
            stage.at[k, 1 - core], relay.at[k], halo_send.at[2], relay_recv.at[k], mate
        )

    def forward_halo(k):
        return remote(
            relay.at[k], ext[k].at[pl.ds(count + core * halo, halo)],
            forward_send, halo_recv.at[k], at(onward, x, core),
        )

    def half_rows(i):
        return pl.ds(i * half, half)

    def pair_copy(k, i):
        rows = half_rows(i) if k == last else pl.ds(0, 2 * half)
        return remote(
            pair_out.at[k, rows], pair_in.at[k, rows], pair_send,
            pair_recv.at[k + i if k == last else k], partner,
        )

    def blocks_sent(count, sent):
        moved = stage.at[pl.ds(0, count), 0]
        return remote(moved, moved, sent, halo_recv.at[0], partner)

    def turn_of(k):
        return k if k < EARLY else k - EARLY

    def z_start(k, j):
        target = j
        slot = lax.rem(z - target + 2 * zs - 1, zs)

        @pl.when(target != z)
        def _():
            remote(
                z_out.at[k, pl.ds(target * tall, tall)], z_in.at[k, slot],
                z_send.at[turn_of(k)], z_recv.at[turn_of(k)], at(target, x, core),
            ).start()

    def z_all(k):
        came = z_in.at[k, pl.ds(0, zs - 1)]
        return remote(came, came, z_send.at[turn_of(k)], z_recv.at[turn_of(k)], partner)

    def x_copy(k, which):
        to_x = x if which == 2 else 1 - x
        to_core = core if which == 1 else 1 - core
        slot = 0 if which == 2 else 1
        return remote(
            x_out.at[k, pl.ds(pl.multiple_of((to_x * CORES + to_core) * each, each), each)], x_in.at[k, slot],
            x_send.at[turn_of(k)], x_recv.at[k], at(z, to_x, to_core),
        )

    def far_start(k, i):
        for j in range(zs // 2):
            to_z = i * (zs // 2) + j
            for to_x in range(XS):
                slot = lax.rem(chip - to_z * XS - to_x + 2 * chips - 1, chips)
                for to_core in range(CORES):
                    owner = at(to_z, to_x, to_core)

                    @pl.when(owner != me)
                    def _():
                        remote(
                            z_out.at[k, pl.ds(owner * each, each)],
                            far_in.at[k - hops, slot], far_send,
                            far_recv.at[k - hops], owner,
                        ).start()

    near = [(None, partner), (None, mate), (z > 0, at(z - 1, x, core)), (z < zs - 1, at(z + 1, x, core))]
    near_count = 2 + (z > 0).astype(jnp.int32) + (z < zs - 1).astype(jnp.int32)

    crossing = jnp.logical_and(early, has_outer)
    close = near[:2] + [(crossing, outer)]
    close_count = 2 + crossing.astype(jnp.int32)

    def tell(sem, peers):
        for there, peer in peers:
            if there is None:
                pl.semaphore_signal(sem, inc=1, device_id={"mesh": peer}, device_id_type=MESH)
            else:
                @pl.when(there)
                def _():
                    pl.semaphore_signal(sem, inc=1, device_id={"mesh": peer}, device_id_type=MESH)

    for k in range(chunks):
        local_copy(k, own, own_sem).start()
    barrier = pltpu.get_barrier_semaphore()
    tell(barrier, close)
    ops_copy.start()

    def direct_start(k, here=True):
        @pl.when(jnp.logical_and(jnp.logical_and(crossing, k < chunks - relayed), here))
        def _():
            outer_halo(k).start()

    for k in range(chunks):
        local_copy(k, own, own_sem).wait()
        local_copy(k, ext, own_sem).start()
        for way, first in ((0, halo), (1, 0)):
            for h in range(halo):
                stage[k, way, h] = own[k][sends[0, first + h]]
        if k == 0:
            pl.semaphore_wait(barrier, close_count)
            tell(rounds.at[0], close)

        @pl.when(jnp.logical_and(early, k >= chunks - relayed))
        def _():
            relay_halo(k).start()

        if k in DIRECT[0]:
            direct_start(k)

        if k == 0:
            @pl.when(late)
            def _():
                outer_halo(k).start()
        else:
            @pl.when(jnp.logical_and(late, relayed < GATED))
            def _():
                outer_halo(k).start()
        pair_halo(k).start()

    @pl.when(jnp.logical_not(has_outer))
    def _():
        for k in range(chunks):
            ext[k][pl.ds(count + core * halo, halo)] = jnp.zeros((halo, size, width), jnp.bfloat16)

    pair_rows = 2 * size
    for k in range(chunks):
        def turn(r, carry):
            start = pl.multiple_of(r * pair_rows, pair_rows)
            turned[k * width:(k + 1) * width, pl.ds(start, pair_rows)] = (
                own[k][pl.ds(r * 2, 2)].reshape(pair_rows, width).T
            )
            return carry

        lax.fori_loop(0, count // 2, turn, 0)

    for k in DIRECT[1]:
        direct_start(k)
    for k in DIRECT[2][:3]:
        direct_start(k, relayed == 0)

    for r in range(zs + 1):
        pl.semaphore_wait(rounds.at[r], close_count if r < CLOSE else near_count)
        if r < zs:
            tell(rounds.at[r + 1], close if r + 1 < CLOSE else near)

    ops_copy.wait()
    for k in range(chunks):
        local_copy(k, ext, own_sem).wait()

    def precompute(g, carry):
        row = pl.multiple_of(g * size, size)
        for p in range(params):
            diagonal[pl.ds(row, size), p * width:(p + 1) * width] = jnp.dot(
                ops[p, g, 0], own[last][g], preferred_element_type=jnp.float32
            )
        return carry

    lax.fori_loop(0, count, precompute, 0, unroll=2)

    for i, k in enumerate(DIRECT[2]):
        direct_start(k, relayed > 0 if i < 3 else True)

    def serve(k):
        if k == last:
            for c in range(1, chunks + 1):
                @pl.when(jnp.logical_and(early, relayed == c))
                def _():
                    blocks_sent(c, halo_send.at[2]).wait_send()
                    if c >= GATED:
                        pl.semaphore_signal(
                            go, inc=1, device_id={"mesh": partner}, device_id_type=MESH
                        )

        @pl.when(jnp.logical_and(early, k >= chunks - relaying))
        def _():
            relay_in(k).wait_recv()
            forward_halo(k).start()

    def relay_in(k):
        return remote(relay.at[k], relay.at[k], halo_send.at[2], relay_recv.at[k], mate)

    def compute(k):
        if k == 0:
            both = stage.at[:, core]
            remote(both, both, halo_send.at[0], halo_recv.at[chunks], partner).wait_recv()

        @pl.when(has_outer)
        def _():
            forward_halo(k).wait_recv()

        def apply(g, carry):
            row = pl.multiple_of(g * size, size)
            first = 1 if k == last else 0
            diag = [] if k == last else [ext[k][g]]
            for p in range(params):
                parts = list(diag)
                for s in range(1, slots):
                    parts.append(ext[k][columns[p, s - 1, g]])
                left = jnp.concatenate([ops[p, g, s] for s in range(first, slots)], axis=1)
                made = jnp.dot(
                    left, jnp.concatenate(parts, axis=0), preferred_element_type=jnp.float32
                )
                if k == last:
                    made = made + diagonal[pl.ds(row, size), p * width:(p + 1) * width]
                image[pl.ds(row, size), p * width:(p + 1) * width] = made.astype(jnp.bfloat16)
            return carry

        lax.fori_loop(0, count, apply, 0, unroll=count)
        for i in range(2):
            made = jnp.dot(
                turned[half_rows(i), :], image[...], preferred_element_type=jnp.float32
            )
            part[k, half_rows(i)] = made
            pair_out[k, half_rows(i)] = made.astype(jnp.bfloat16)

            if i == 1 or k == last:
                @pl.when(late if k < EARLY else early)
                def _():
                    pair_copy(k, i).start()

            if k >= EARLY:
                @pl.when(late)
                def _():
                    join(k, i)
                    if k < hops:
                        z_start_half(k, i)
                    else:
                        far_start(k, i)

    def join(k, i):
        if i == 0 or k == last:
            pair_copy(k, i).wait_recv()
        rows = half_rows(i)
        total = part[k, rows] + pair_in[k, rows].astype(jnp.float32)
        part[k, rows] = total
        z_out[k, rows] = total.astype(jnp.bfloat16)

    def z_start_half(k, i):
        if i == 0:
            for j in range(zs // 2):
                z_start(k, j)
        else:
            for j in range(zs // 2, zs):
                z_start(k, j)

    def gather(k):
        for i in range(2):
            join(k, i)
        for j in range(zs):
            z_start(k, j)

    def across(k):
        total = part[k, pl.ds(pl.multiple_of(z * tall, tall), tall)]
        z_all(k).wait_recv()
        for s in range(1, zs):
            total = total + z_in[k, s - 1].astype(jnp.float32)
        x_own[k] = total
        x_out[k] = total.astype(jnp.bfloat16)
        for which in range(3):
            x_copy(k, which).start()

    def put(k, total):
        for p in range(params):
            out[:, p * basis_width + k * width:p * basis_width + (k + 1) * width] = total[
                :, p * width:(p + 1) * width
            ]

    def finish_staged(k, mine):
        came = x_in.at[k, pl.ds(1 if mine else 0, 1 if mine else 2)]
        remote(came, came, x_send.at[0], x_recv.at[k], partner).wait_recv()
        if mine:
            first = x_own[k, pl.ds(pl.multiple_of((x * CORES + core) * each, each), each)]
        else:
            first = x_in[k, 0].astype(jnp.float32)
        put(k, first + x_in[k, 1].astype(jnp.float32))

    def finish_far(k, mine):
        if mine:
            total = part[k, pl.ds(pl.multiple_of(me * each, each), each)]
        else:
            total = jnp.zeros((each, params * width), jnp.float32)
        came = chips - 1 if mine else chips
        remote(
            far_in.at[k - hops, pl.ds(0, came)], far_in.at[k - hops, pl.ds(0, came)],
            far_send, far_recv.at[k - hops], partner,
        ).wait_recv()
        for s in range(came):
            total = total + far_in[k - hops, s].astype(jnp.float32)
        put(k, total)

    def finish(k, mine):
        if k < hops:
            finish_staged(k, mine)
        else:
            finish_far(k, mine)

    def ungate():
        @pl.when(jnp.logical_and(late, relayed >= GATED))
        def _():
            pl.semaphore_wait(go, 1)
            for k in range(1, chunks):
                outer_halo(k).start()

    for k in range(min(SERVED + 1, chunks)):
        serve(k)
    for k in range(chunks):
        compute(k)
        if k + SERVED + 1 < chunks:
            serve(k + SERVED + 1)
        if k == 0:
            ungate()
        if k + 3 < len(DIRECT):
            for later in DIRECT[k + 3]:
                direct_start(later)
        if 0 <= k - LAG < EARLY:
            @pl.when(early)
            def _():
                gather(k - LAG)
        if EARLY <= k - SLACK < hops:
            @pl.when(late)
            def _():
                across(k - SLACK)

    @pl.when(early)
    def _():
        for k in range(EARLY):
            across(k)
        for k in range(chunks):
            finish(k, k < EARLY)

    @pl.when(late)
    def _():
        for k in range(chunks):
            finish(k, k >= EARLY)

    blocks_sent(chunks, halo_send.at[0]).wait_send()

    @pl.when(late)
    def _():
        blocks_sent(chunks, halo_send.at[1]).wait_send()

    for c in range(1, chunks + 1):
        @pl.when(jnp.logical_and(crossing, relayed == chunks - c))
        def _():
            blocks_sent(c, halo_send.at[1]).wait_send()

        @pl.when(jnp.logical_and(early, relaying == c))
        def _():
            blocks_sent(c, forward_send).wait_send()

    def sums_sent(first, end):
        summed = pair_out.at[pl.ds(first, end - first)]
        remote(summed, summed, pair_send, pair_recv.at[0], partner).wait_send()

    def staged_sent(k):
        z_all(k).wait_send()
        rows = x_out.at[k, pl.ds(0, 3 * each)]
        remote(rows, rows, x_send.at[turn_of(k)], x_recv.at[k], partner).wait_send()

    @pl.when(early)
    def _():
        sums_sent(EARLY, chunks)
        for k in range(EARLY):
            staged_sent(k)

    @pl.when(late)
    def _():
        sums_sent(0, EARLY)
        for k in range(EARLY, hops):
            staged_sent(k)
        rows = z_out.at[pl.ds(hops, chunks - hops), pl.ds(0, (n - 1) * each)]
        remote(rows, rows, far_send, far_recv.at[0], partner).wait_send()


def relays_out(zs, chunks, z, x):
    if x == 1:
        return jnp.where(z < zs - 1, jnp.clip(chunks - 1 - z, 0, chunks), 0)
    return jnp.clip(z - 1, 0, chunks)


def fused_shards(n, basis, blocks, columns, sends):
    params, count, slots, size, _ = blocks.shape
    rows, basis_width = basis.shape
    halo = sends.shape[1] // 2
    zs = n // (CORES * XS)
    width = LANES
    chunks = basis_width // width
    each = basis_width // n
    tall = XS * CORES * each
    bf, f32 = jnp.bfloat16, jnp.float32
    wide = params * width
    dma = pltpu.SemaphoreType.DMA
    hops = chunks - FAR
    turns = max(EARLY, hops - EARLY)
    return pl.pallas_call(
        functools.partial(kernel, n, zs, width),
        out_shape=pltpu.VMEM((each, params * basis_width), f32),
        in_specs=[
            pl.BlockSpec(memory_space=pl.ANY),
            pl.BlockSpec(memory_space=pl.ANY),
            pl.BlockSpec(memory_space=pltpu.SMEM),
            pl.BlockSpec(memory_space=pltpu.SMEM),
        ],
        out_specs=pl.BlockSpec(memory_space=pltpu.VMEM),
        scratch_shapes=[pltpu.VMEM((count, size, width), bf) for _ in range(chunks)]
        + [pltpu.VMEM((count + 2 * halo, size, width), bf) for _ in range(chunks)]
        + [
            pltpu.VMEM((chunks, 2, halo, size, width), bf),
            pltpu.VMEM((chunks, halo, size, width), bf),
            pltpu.VMEM((basis_width, rows), bf),
            pltpu.VMEM(blocks.shape, bf),
            pltpu.VMEM((rows, wide), f32),
            pltpu.VMEM((rows, wide), bf),
            pltpu.VMEM((chunks, basis_width, wide), f32),
            pltpu.VMEM((chunks, basis_width, wide), bf),
            pltpu.VMEM((chunks, basis_width, wide), bf),
            pltpu.VMEM((chunks, basis_width, wide), bf),
            pltpu.VMEM((hops, zs, tall, wide), bf),
            pltpu.VMEM((hops, tall, wide), f32),
            pltpu.VMEM((hops, tall, wide), bf),
            pltpu.VMEM((hops, 2, each, wide), bf),
            pltpu.VMEM((chunks - hops, n // CORES, each, wide), bf),
            dma((chunks,)),
            dma,
            dma((3,)),
            dma((chunks + 1,)),
            dma((chunks,)),
            dma,
            dma,
            dma((chunks + 1,)),
            dma((turns,)),
            dma((turns,)),
            dma((turns,)),
            dma((hops,)),
            dma,
            dma((chunks - hops,)),
            pltpu.SemaphoreType.REGULAR((zs + 1,)),
            pltpu.SemaphoreType.REGULAR,
        ],
        compiler_params=pltpu.CompilerParams(collective_id=0, has_side_effects=True),
    )(basis.reshape(count, size, basis_width), blocks, jnp.swapaxes(columns, 1, 2), sends)


def solution(mesh):
    n = mesh.shape["mesh"]

    def shards(basis, blocks, columns, sends):
        each = basis.shape[1] // n
        tiled = basis.shape[1] % (n * 16) == 0 and LANES % max(each, 1) == 0
        chunked = basis.shape[1] // LANES >= EARLY + FAR and n % (2 * XS * CORES) == 0
        if chunked and tiled and blocks.shape[3] == LANES:
            return fused_shards(n, basis, blocks, columns, sends)
        return plain_shards(basis, blocks, columns, sends)

    placed = (
        P(("grp", "mesh"), None),
        P(None, ("grp", "mesh"), None, None, None),
        P(None, ("grp", "mesh"), None),
        P(("grp", "mesh"), None),
    )
    return jax.shard_map(
        shards, mesh=mesh, in_specs=placed, out_specs=P(("grp", "mesh"), None), check_vma=False
    )
```

```python
import functools

import jax
import jax.numpy as jnp
from jax import lax
from jax.experimental import pallas as pl
from jax.experimental.pallas import tpu as pltpu
from jax.sharding import PartitionSpec as P

MESH = pl.DeviceIdType.MESH
CORES = 2
LANES = 128
XS = 2
EARLY = 1
FAR = 2
SERVED = 2
LAG = 0
DIRECT = ((), (0,), (1, 2, 3))
SLACK = 2
CLOSE = 3
GATED = 2


def from_behind(value, axis, steps):
    count = lax.axis_size(axis)
    leading, last = (max(0, -steps), min(count, count - steps))
    return lax.ppermute(value, axis, [(source, source + steps) for source in range(leading, last)])


def plain_shards(basis, blocks, columns, sends):
    count_params, count_blocks, count_slots, block_size, _ = blocks.shape
    basis_width = basis.shape[1]
    halo_count = sends.shape[1] // 2
    own_blocks = basis.reshape(count_blocks, block_size, basis_width)
    diag_index = jnp.arange(count_blocks, dtype=jnp.int32)[:, None]
    images = []
    upward = jnp.take(own_blocks, sends[0, halo_count:], axis=0)
    downward = jnp.take(own_blocks, sends[0, :halo_count], axis=0)
    from_below = from_behind(upward, "mesh", 1)
    from_above = from_behind(downward, "mesh", -1)
    extended = jnp.concatenate([own_blocks, from_below, from_above], axis=0)
    for param in range(count_params):
        slot_index = jnp.concatenate([diag_index, columns[param]], axis=1)
        gathered = jnp.take(extended, slot_index, axis=0)
        accumulated = jnp.einsum(
            "bsik,bskj->bij", blocks[param], gathered, preferred_element_type=jnp.float32
        )
        images.append(
            accumulated.astype(jnp.bfloat16).reshape(count_blocks * block_size, basis_width)
        )
    stacked_images = jnp.concatenate(images, axis=1)
    return lax.psum_scatter(
        lax.dot_general(
            basis, stacked_images, (((0,), (0,)), ((), ())), preferred_element_type=jnp.float32
        ),
        "mesh",
        scatter_dimension=0,
        tiled=True,
    )


def kernel(n, zs, width, basis, blocks, columns_there, sends_there, out, *scratch):
    chunks = basis.shape[2] // width
    own, scratch = scratch[:chunks], scratch[chunks:]
    ext, scratch = scratch[:chunks], scratch[chunks:]
    (
        stage, relay, turned, ops, diagonal, image, part, pair_out, pair_in, z_out, z_in, x_own, x_out, x_in,
        far_in, columns, sends, table_sem, own_sem, ops_sem, halo_send, halo_recv, relay_recv, forward_send,
        pair_send, pair_recv, z_send, z_recv, x_send, x_recv, far_send, far_recv, rounds, go,
    ) = scratch
    params, count, slots, size, _ = blocks.shape
    basis_width = basis.shape[2]
    halo = sends.shape[1] // 2
    half = basis_width // 2
    each = basis_width // n
    chips = n // CORES
    plane = XS * CORES
    tall = plane * each
    last = chunks - 1
    hops = chunks - FAR

    me = lax.axis_index("mesh")
    core = lax.rem(me, CORES)
    chip = me // CORES
    x = lax.rem(chip, XS)
    z = chip // XS
    early = core == x
    late = core != x

    def at(z, x, core):
        return (z * XS + x) * CORES + core

    partner = at(z, x, 1 - core)
    mate = at(z, 1 - x, 1 - core)
    outer = me - 1 + 2 * core
    has_outer = jnp.logical_and(outer >= 0, outer < n)
    onward = z + 1 - 2 * x
    relayed = (
        relays_out(zs, chunks, z, 1) * x + relays_out(zs, chunks, z, 0) * (1 - x)
    )
    relaying = (
        relays_out(zs, chunks, z, 0) * x + relays_out(zs, chunks, z, 1) * (1 - x)
    )

    def local_copy(k, buffers, sems):
        return pltpu.make_async_copy(
            basis.at[:, :, pl.ds(k * width, width)], buffers[k].at[pl.ds(0, count)], sems.at[k]
        )

    ops_copy = pltpu.make_async_copy(blocks, ops, ops_sem)

    def remote(source, target, sent, received, device):
        return pltpu.make_async_remote_copy(
            src_ref=source, dst_ref=target, send_sem=sent, recv_sem=received,
            device_id={"mesh": device}, device_id_type=MESH,
        )

    def pair_halo(k):
        return remote(
            stage.at[k, core], ext[k].at[pl.ds(count + core * halo, halo)],
            halo_send.at[0], halo_recv.at[chunks], partner,
        )

    def outer_halo(k):
        return remote(
            stage.at[k, 1 - core], ext[k].at[pl.ds(count + (1 - core) * halo, halo)],
            halo_send.at[1], halo_recv.at[k], outer,
        )

    def relay_halo(k):
        return remote(
            stage.at[k, 1 - core], relay.at[k], halo_send.at[2], relay_recv.at[k], mate
        )

    def forward_halo(k):
        return remote(
            relay.at[k], ext[k].at[pl.ds(count + core * halo, halo)],
            forward_send, halo_recv.at[k], at(onward, x, core),
        )

    def half_rows(i):
        return pl.ds(i * half, half)

    def pair_copy(k, i):
        rows = half_rows(i) if k == last else pl.ds(0, 2 * half)
        return remote(
            pair_out.at[k, rows], pair_in.at[k, rows], pair_send,
            pair_recv.at[k + i if k == last else k], partner,
        )

    def blocks_sent(count, sent):
        moved = stage.at[pl.ds(0, count), 0]
        return remote(moved, moved, sent, halo_recv.at[0], partner)

    def turn_of(k):
        return k if k < EARLY else k - EARLY

    def z_start(k, j):
        target = j
        slot = lax.rem(z - target + 2 * zs - 1, zs)

        @pl.when(target != z)
        def _():
            remote(
                z_out.at[k, pl.ds(target * tall, tall)], z_in.at[k, slot],
                z_send.at[turn_of(k)], z_recv.at[turn_of(k)], at(target, x, core),
            ).start()

    def z_all(k):
        came = z_in.at[k, pl.ds(0, zs - 1)]
        return remote(came, came, z_send.at[turn_of(k)], z_recv.at[turn_of(k)], partner)

    def x_copy(k, which):
        to_x = x if which == 2 else 1 - x
        to_core = core if which == 1 else 1 - core
        slot = 0 if which == 2 else 1
        return remote(
            x_out.at[k, pl.ds(pl.multiple_of((to_x * CORES + to_core) * each, each), each)], x_in.at[k, slot],
            x_send.at[turn_of(k)], x_recv.at[k], at(z, to_x, to_core),
        )

    def far_start(k, i):
        for j in range(zs // 2):
            to_z = i * (zs // 2) + j
            for to_x in range(XS):
                slot = lax.rem(chip - to_z * XS - to_x + 2 * chips - 1, chips)
                for to_core in range(CORES):
                    owner = at(to_z, to_x, to_core)

                    @pl.when(owner != me)
                    def _():
                        remote(
                            z_out.at[k, pl.ds(owner * each, each)],
                            far_in.at[k - hops, slot], far_send,
                            far_recv.at[k - hops], owner,
                        ).start()

    near = [(None, partner), (None, mate), (z > 0, at(z - 1, x, core)), (z < zs - 1, at(z + 1, x, core))]
    near_count = 2 + (z > 0).astype(jnp.int32) + (z < zs - 1).astype(jnp.int32)

    crossing = jnp.logical_and(early, has_outer)
    close = near[:2] + [(crossing, outer)]
    close_count = 2 + crossing.astype(jnp.int32)

    def tell(sem, peers):
        for there, peer in peers:
            if there is None:
                pl.semaphore_signal(sem, inc=1, device_id={"mesh": peer}, device_id_type=MESH)
            else:
                @pl.when(there)
                def _():
                    pl.semaphore_signal(sem, inc=1, device_id={"mesh": peer}, device_id_type=MESH)

    sends_copy = pltpu.make_async_copy(sends_there, sends, table_sem.at[0])
    columns_copy = pltpu.make_async_copy(columns_there, columns, table_sem.at[1])
    sends_copy.start()
    for k in range(chunks):
        local_copy(k, own, own_sem).start()
    barrier = pltpu.get_barrier_semaphore()
    tell(barrier, close)
    columns_copy.start()
    ops_copy.start()

    sends_copy.wait()

    def direct_start(k, here=True):
        @pl.when(jnp.logical_and(jnp.logical_and(crossing, k < chunks - relayed), here))
        def _():
            outer_halo(k).start()

    for k in range(chunks):
        local_copy(k, own, own_sem).wait()
        local_copy(k, ext, own_sem).start()
        for way, first in ((0, halo), (1, 0)):
            for h in range(halo):
                stage[k, way, h] = own[k][sends[0, first + h]]
        if k == 0:
            pl.semaphore_wait(barrier, close_count)
            tell(rounds.at[0], close)

        @pl.when(jnp.logical_and(early, k >= chunks - relayed))
        def _():
            relay_halo(k).start()

        if k in DIRECT[0]:
            direct_start(k)

        if k == 0:
            @pl.when(late)
            def _():
                outer_halo(k).start()
        else:
            @pl.when(jnp.logical_and(late, relayed < GATED))
            def _():
                outer_halo(k).start()
        pair_halo(k).start()

    @pl.when(jnp.logical_not(has_outer))
    def _():
        for k in range(chunks):
            ext[k][pl.ds(count + core * halo, halo)] = jnp.zeros((halo, size, width), jnp.bfloat16)

    pair_rows = 2 * size
    for k in range(chunks):
        def turn(r, carry):
            start = pl.multiple_of(r * pair_rows, pair_rows)
            turned[k * width:(k + 1) * width, pl.ds(start, pair_rows)] = (
                own[k][pl.ds(r * 2, 2)].reshape(pair_rows, width).T
            )
            return carry

        lax.fori_loop(0, count // 2, turn, 0)

    for k in DIRECT[1]:
        direct_start(k)
    for k in DIRECT[2][:3]:
        direct_start(k, relayed <= (1 - x if k == 1 else 0))

    for r in range(zs + 1):
        pl.semaphore_wait(rounds.at[r], close_count if r < CLOSE else near_count)
        if r < zs:
            tell(rounds.at[r + 1], close if r + 1 < CLOSE else near)

    columns_copy.wait()
    ops_copy.wait()
    for k in range(chunks):
        local_copy(k, ext, own_sem).wait()

    def precompute(g, carry):
        row = pl.multiple_of(g * size, size)
        for p in range(params):
            diagonal[pl.ds(row, size), p * width:(p + 1) * width] = jnp.dot(
                ops[p, g, 0], own[last][g], preferred_element_type=jnp.float32
            )
        return carry

    lax.fori_loop(0, count, precompute, 0, unroll=2)

    for i, k in enumerate(DIRECT[2]):
        direct_start(k, relayed > (1 - x if k == 1 else 0) if i < 3 else True)

    def serve(k):
        if k == last:
            for c in range(1, chunks + 1):
                @pl.when(jnp.logical_and(early, relayed == c))
                def _():
                    blocks_sent(c, halo_send.at[2]).wait_send()
                    if c >= GATED:
                        pl.semaphore_signal(
                            go, inc=1, device_id={"mesh": partner}, device_id_type=MESH
                        )

        @pl.when(jnp.logical_and(early, k >= chunks - relaying))
        def _():
            relay_in(k).wait_recv()
            forward_halo(k).start()

    def relay_in(k):
        return remote(relay.at[k], relay.at[k], halo_send.at[2], relay_recv.at[k], mate)

    def compute(k):
        if k == 0:
            both = stage.at[:, core]
            remote(both, both, halo_send.at[0], halo_recv.at[chunks], partner).wait_recv()

        @pl.when(has_outer)
        def _():
            forward_halo(k).wait_recv()

        def apply(g, carry):
            row = pl.multiple_of(g * size, size)
            first = 1 if k == last else 0
            diag = [] if k == last else [ext[k][g]]
            for p in range(params):
                parts = list(diag)
                for s in range(1, slots):
                    parts.append(ext[k][columns[p, s - 1, g]])
                left = jnp.concatenate([ops[p, g, s] for s in range(first, slots)], axis=1)
                made = jnp.dot(
                    left, jnp.concatenate(parts, axis=0), preferred_element_type=jnp.float32
                )
                if k == last:
                    made = made + diagonal[pl.ds(row, size), p * width:(p + 1) * width]
                image[pl.ds(row, size), p * width:(p + 1) * width] = made.astype(jnp.bfloat16)
            return carry

        lax.fori_loop(0, count, apply, 0, unroll=count)
        for i in range(2):
            made = jnp.dot(
                turned[half_rows(i), :], image[...], preferred_element_type=jnp.float32
            )
            part[k, half_rows(i)] = made
            pair_out[k, half_rows(i)] = made.astype(jnp.bfloat16)

            if i == 1 or k == last:
                @pl.when(late if k < EARLY else early)
                def _():
                    pair_copy(k, i).start()

            if k >= EARLY:
                @pl.when(late)
                def _():
                    join(k, i)
                    if k < hops:
                        z_start_half(k, i)
                    else:
                        far_start(k, i)

    def join(k, i):
        if i == 0 or k == last:
            pair_copy(k, i).wait_recv()
        rows = half_rows(i)
        total = part[k, rows] + pair_in[k, rows].astype(jnp.float32)
        part[k, rows] = total
        z_out[k, rows] = total.astype(jnp.bfloat16)

    def z_start_half(k, i):
        if i == 0:
            for j in range(zs // 2):
                z_start(k, j)
        else:
            for j in range(zs // 2, zs):
                z_start(k, j)

    def gather(k):
        for i in range(2):
            join(k, i)
        for j in range(zs):
            z_start(k, j)

    def across(k):
        total = part[k, pl.ds(pl.multiple_of(z * tall, tall), tall)]
        z_all(k).wait_recv()
        for s in range(1, zs):
            total = total + z_in[k, s - 1].astype(jnp.float32)
        x_own[k] = total
        x_out[k] = total.astype(jnp.bfloat16)
        for which in range(3):
            x_copy(k, which).start()

    def put(k, total):
        for p in range(params):
            out[:, p * basis_width + k * width:p * basis_width + (k + 1) * width] = total[
                :, p * width:(p + 1) * width
            ]

    def finish_staged(k, mine):
        came = x_in.at[k, pl.ds(1 if mine else 0, 1 if mine else 2)]
        remote(came, came, x_send.at[0], x_recv.at[k], partner).wait_recv()
        if mine:
            first = x_own[k, pl.ds(pl.multiple_of((x * CORES + core) * each, each), each)]
        else:
            first = x_in[k, 0].astype(jnp.float32)
        put(k, first + x_in[k, 1].astype(jnp.float32))

    def finish_far(k, mine):
        if mine:
            total = part[k, pl.ds(pl.multiple_of(me * each, each), each)]
        else:
            total = jnp.zeros((each, params * width), jnp.float32)
        came = chips - 1 if mine else chips
        remote(
            far_in.at[k - hops, pl.ds(0, came)], far_in.at[k - hops, pl.ds(0, came)],
            far_send, far_recv.at[k - hops], partner,
        ).wait_recv()
        for s in range(came):
            total = total + far_in[k - hops, s].astype(jnp.float32)
        put(k, total)

    def finish(k, mine):
        if k < hops:
            finish_staged(k, mine)
        else:
            finish_far(k, mine)

    def ungate():
        @pl.when(jnp.logical_and(late, relayed >= GATED))
        def _():
            pl.semaphore_wait(go, 1)
            for k in range(1, chunks):
                outer_halo(k).start()

    for k in range(min(SERVED + 1, chunks)):
        serve(k)
    for k in range(chunks):
        compute(k)
        if k + SERVED + 1 < chunks:
            serve(k + SERVED + 1)
        if k == 0:
            ungate()
        if k + 3 < len(DIRECT):
            for later in DIRECT[k + 3]:
                direct_start(later)
        if 0 <= k - LAG < EARLY:
            @pl.when(early)
            def _():
                gather(k - LAG)
        if EARLY <= k - SLACK < hops:
            @pl.when(late)
            def _():
                across(k - SLACK)

    @pl.when(early)
    def _():
        for k in range(EARLY):
            across(k)
        for k in range(chunks):
            finish(k, k < EARLY)

    @pl.when(late)
    def _():
        for k in range(chunks):
            finish(k, k >= EARLY)

    blocks_sent(chunks, halo_send.at[0]).wait_send()

    @pl.when(late)
    def _():
        blocks_sent(chunks, halo_send.at[1]).wait_send()

    for c in range(1, chunks + 1):
        @pl.when(jnp.logical_and(crossing, relayed == chunks - c))
        def _():
            blocks_sent(c, halo_send.at[1]).wait_send()

        @pl.when(jnp.logical_and(early, relaying == c))
        def _():
            blocks_sent(c, forward_send).wait_send()

    def sums_sent(first, end):
        summed = pair_out.at[pl.ds(first, end - first)]
        remote(summed, summed, pair_send, pair_recv.at[0], partner).wait_send()

    def staged_sent(k):
        z_all(k).wait_send()
        rows = x_out.at[k, pl.ds(0, 3 * each)]
        remote(rows, rows, x_send.at[turn_of(k)], x_recv.at[k], partner).wait_send()

    @pl.when(early)
    def _():
        sums_sent(EARLY, chunks)
        for k in range(EARLY):
            staged_sent(k)

    @pl.when(late)
    def _():
        sums_sent(0, EARLY)
        for k in range(EARLY, hops):
            staged_sent(k)
        rows = z_out.at[pl.ds(hops, chunks - hops), pl.ds(0, (n - 1) * each)]
        remote(rows, rows, far_send, far_recv.at[0], partner).wait_send()


def relays_out(zs, chunks, z, x):
    if x == 1:
        return jnp.where(z < zs - 1, jnp.clip(chunks - 1 - z, 0, chunks), 0)
    return jnp.clip(z - 1, 0, chunks)


def fused_shards(n, basis, blocks, columns, sends):
    params, count, slots, size, _ = blocks.shape
    rows, basis_width = basis.shape
    halo = sends.shape[1] // 2
    zs = n // (CORES * XS)
    width = LANES
    chunks = basis_width // width
    each = basis_width // n
    tall = XS * CORES * each
    bf, f32 = jnp.bfloat16, jnp.float32
    wide = params * width
    dma = pltpu.SemaphoreType.DMA
    hops = chunks - FAR
    turns = max(EARLY, hops - EARLY)
    return pl.pallas_call(
        functools.partial(kernel, n, zs, width),
        out_shape=pltpu.VMEM((each, params * basis_width), f32),
        in_specs=[
            pl.BlockSpec(memory_space=pl.ANY),
            pl.BlockSpec(memory_space=pl.ANY),
            pl.BlockSpec(memory_space=pl.ANY),
            pl.BlockSpec(memory_space=pl.ANY),
        ],
        out_specs=pl.BlockSpec(memory_space=pltpu.VMEM),
        scratch_shapes=[pltpu.VMEM((count, size, width), bf) for _ in range(chunks)]
        + [pltpu.VMEM((count + 2 * halo, size, width), bf) for _ in range(chunks)]
        + [
            pltpu.VMEM((chunks, 2, halo, size, width), bf),
            pltpu.VMEM((chunks, halo, size, width), bf),
            pltpu.VMEM((basis_width, rows), bf),
            pltpu.VMEM(blocks.shape, bf),
            pltpu.VMEM((rows, wide), f32),
            pltpu.VMEM((rows, wide), bf),
            pltpu.VMEM((chunks, basis_width, wide), f32),
            pltpu.VMEM((chunks, basis_width, wide), bf),
            pltpu.VMEM((chunks, basis_width, wide), bf),
            pltpu.VMEM((chunks, basis_width, wide), bf),
            pltpu.VMEM((hops, zs, tall, wide), bf),
            pltpu.VMEM((hops, tall, wide), f32),
            pltpu.VMEM((hops, tall, wide), bf),
            pltpu.VMEM((hops, 2, each, wide), bf),
            pltpu.VMEM((chunks - hops, n // CORES, each, wide), bf),
            pltpu.SMEM((params, slots - 1, count), jnp.int32),
            pltpu.SMEM((1, 2 * halo), jnp.int32),
            dma((2,)),
            dma((chunks,)),
            dma,
            dma((3,)),
            dma((chunks + 1,)),
            dma((chunks,)),
            dma,
            dma,
            dma((chunks + 1,)),
            dma((turns,)),
            dma((turns,)),
            dma((turns,)),
            dma((hops,)),
            dma,
            dma((chunks - hops,)),
            pltpu.SemaphoreType.REGULAR((zs + 1,)),
            pltpu.SemaphoreType.REGULAR,
        ],
        compiler_params=pltpu.CompilerParams(collective_id=0, has_side_effects=True),
    )(basis.reshape(count, size, basis_width), blocks, jnp.swapaxes(columns, 1, 2), sends)


def solution(mesh):
    n = mesh.shape["mesh"]

    def shards(basis, blocks, columns, sends):
        each = basis.shape[1] // n
        tiled = basis.shape[1] % (n * 16) == 0 and LANES % max(each, 1) == 0
        chunked = basis.shape[1] // LANES >= EARLY + FAR and n % (2 * XS * CORES) == 0
        if chunked and tiled and blocks.shape[3] == LANES:
            return fused_shards(n, basis, blocks, columns, sends)
        return plain_shards(basis, blocks, columns, sends)

    placed = (
        P(("grp", "mesh"), None),
        P(None, ("grp", "mesh"), None, None, None),
        P(None, ("grp", "mesh"), None),
        P(("grp", "mesh"), None),
    )
    return jax.shard_map(
        shards, mesh=mesh, in_specs=placed, out_specs=P(("grp", "mesh"), None), check_vma=False
    )
```
